256 devices in a mesh: grp: 8 (over x, core), dev: 32 (over y, z).
Axes of the slice: x: 4, y: 4, z: 8, core: 2. Of those that a mesh axis runs over, the one named last changes fastest.
Arguments:
- tensor_slab: bfloat16 [512, 512, 64, 64], P(None, 'dev', 'grp'), may hold values from -400 to 400
- mode_factor: bfloat16 [512, 64], replicated, may hold values from -40 to 40
Outputs:
- triangle: float32 [512, 512], P('dev', 'grp')
The draws below stay inside these ranges and needn't reach their ends.
All inputs are finite; a program needn't handle non-finite values.
Results may differ from the reference program's by a relative error of at most 0.00033.
Values may be sent and summed in bfloat16 or wider, within the bound.
A program may use at most 64 MiB of HBM per device.

```python
import jax
import jax.numpy as jnp
from jax import lax

N1 = 512
N2 = 512
R1 = 64
S = 64
NZ = 64
ROWS = 262144


def draw_tensor_slab(key, part):
    key_list = jax.random.split(jax.random.fold_in(key, 11), 6)
    noise = jnp.clip(jax.random.normal(key_list[0], (N1, N2, NZ, S), jnp.float32), -6.0, 6.0)
    common = jnp.clip(jax.random.normal(key_list[1], (N1, 1, NZ, S), jnp.float32), -6.0, 6.0)
    loading = jnp.clip(0.7 * jax.random.normal(key_list[2], (N2,), jnp.float32), -2.0, 2.0)
    column_scale = jnp.exp(jax.random.uniform(key_list[3], (N2,), jnp.float32, jnp.log(0.3), jnp.log(3.0)))
    depth_scale = (1.0 + 2.0 * jnp.arange(NZ, dtype=jnp.float32) / NZ) * jnp.exp(jax.random.uniform(key_list[4], (NZ,), jnp.float32, jnp.log(0.5), jnp.log(2.0)))
    species_scale = jnp.exp(jax.random.uniform(key_list[5], (S,), jnp.float32, jnp.log(0.5), jnp.log(2.0)))
    values = column_scale[None, :, None, None] * (noise + loading[None, :, None, None] * common)
    values = values * depth_scale[None, None, :, None] * species_scale[None, None, None, :]
    return values.astype(jnp.bfloat16)


def draw_mode_factor(key, part):
    key_list = jax.random.split(jax.random.fold_in(key, 23), 2)
    entries = jnp.clip(jax.random.normal(key_list[0], (N1, R1), jnp.float32), -6.0, 6.0)
    rank_scale = (1.0 + 2.0 * jnp.arange(R1, dtype=jnp.float32) / R1) * jnp.exp(jax.random.uniform(key_list[1], (R1,), jnp.float32, jnp.log(0.5), jnp.log(2.0)))
    return (entries * rank_scale[None, :] / jnp.sqrt(jnp.float32(N1))).astype(jnp.bfloat16)


def setup_inputs(seed: int = 0) -> dict:
    streams_of = jax.random.split(jax.random.key(seed), 3)
    return {
        "tensor_slab": draw_tensor_slab(jax.random.fold_in(streams_of[2], 71), 0),
        "mode_factor": draw_mode_factor(jax.random.fold_in(streams_of[2], 71), 0),
    }


def reference(tensor_slab, mode_factor):
    factor_wide = mode_factor.astype(jnp.float32)

    def absorb(running, slab_index):
        slab_piece = lax.dynamic_index_in_dim(tensor_slab, slab_index, 2, keepdims=False).astype(jnp.float32)
        projected = jnp.einsum('ir,ijs->rsj', factor_wide, slab_piece, precision=lax.Precision.HIGHEST)
        projected = projected.astype(jnp.bfloat16).reshape(R1 * S, N2)
        return (running + jnp.dot(projected.T.astype(jnp.float32), projected.astype(jnp.float32), preferred_element_type=jnp.float32), None)
    gram_total, unused_out = lax.scan(absorb, jnp.zeros((N2, N2), jnp.float32), jnp.arange(NZ, dtype=jnp.int32))
    lower_tri = jnp.linalg.cholesky(gram_total / ROWS)
    return lower_tri.T
```

```python
import functools

import jax
import jax.numpy as jnp
from jax import lax
from jax.experimental import pallas as pl
from jax.experimental.pallas import tpu as pltpu
from jax.sharding import PartitionSpec as P

MESH = pl.DeviceIdType.MESH
BLK = 128
NY = 4


def gram_body(cfg, tt_ref, ft_ref, out_ref, tb, pf, sb, xb, gp, rc, hb, rx, zb, rz, gf,
              ld_sem, sa_sem, ra_sem, sc_sem, rc_sem, sx_sem, rx_sem, sz_sem, rz_sem, sg_sem, rg_sem):
    nx, ny, nz, jl, scale = cfg
    half = gp.shape[0] // 2
    nq = nx * ny
    rows = half // nq
    g = lax.axis_index("grp")
    d = lax.axis_index("dev")
    x, c = g // 2, g % 2
    y, z = d // nz, d % nz
    q_own = x * ny + y

    def dev_id(gg, dd):
        return {"grp": gg, "dev": dd}

    chunks = []
    for t in range(ny):
        cg = (y + 1 + t) % ny
        cp = pltpu.make_async_copy(tt_ref.at[:, pl.ds(pl.multiple_of(cg * BLK, BLK), BLK), :], tb.at[t], ld_sem.at[t])
        cp.start()
        chunks.append(cp)

    barrier = pltpu.get_barrier_semaphore()
    nbar = 0

    def sig(gg, dd):
        pl.semaphore_signal(barrier, inc=1, device_id=dev_id(gg, dd), device_id_type=MESH)

    for k in range(1, ny * nz):
        sig(g, (d + k) % (ny * nz))
        nbar += 1
    for kx in range(1, nx):
        for ky in range(ny):
            sig(((x + kx) % nx) * 2 + c, ((y + ky) % ny) * nz + z)
            nbar += 1
    sig(x * 2 + 1 - c, d)
    nbar += 1

    zorder = sorted(range(nz), key=lambda k: (-min(k, nz - k), k))
    mine = pl.ds(pl.multiple_of(d * jl, jl), jl)
    jg = 256 // BLK
    sends = []
    for t in range(ny):
        chunks[t].wait()

        def proj(i, carry):
            rhs = tb[t, pl.ds(i * jg, jg)].reshape(jg * BLK, tb.shape[-1])
            o = lax.dot_general(ft_ref[...], rhs, (((1,), (1,)), ((), ())), preferred_element_type=jnp.float32)
            for rg in range(nz):
                for jj in range(jg):
                    pf[pl.ds(pl.multiple_of(rg * jl * 8 + (i * jg + jj) * 8, 8), 8), :] = o[rg * 8:(rg + 1) * 8, jj * BLK:(jj + 1) * BLK]
            return carry

        lax.fori_loop(0, jl // jg, proj, 0)
        cg = (y + 1 + t) % ny
        for n, zo in enumerate(zorder):
            rg = (z + zo) % nz
            local = t == ny - 1 and zo == 0
            for r in range(8):
                v = pf[pl.ds(pl.multiple_of(rg * jl * 8, 8) + r, jl, stride=8), :].astype(jnp.bfloat16)
                if local:
                    xb[mine, r * BLK:(r + 1) * BLK] = v
                else:
                    sb[t, n, :, r * BLK:(r + 1) * BLK] = v
            if t == 0 and n == 0:
                pl.semaphore_wait(barrier, nbar)
            if not local:
                cp = pltpu.make_async_remote_copy(sb.at[t, n], xb.at[mine, :], sa_sem.at[t, n], ra_sem.at[d],
                                                  device_id=dev_id(g, cg * nz + rg), device_id_type=MESH)
                cp.start()
                sends.append(cp)

    def wait_src(k, carry):
        src = (d + k) % (ny * nz)
        blk = xb.at[pl.ds(pl.multiple_of(src * jl, jl), jl), :]
        pltpu.make_async_copy(blk, blk, ra_sem.at[src]).wait()
        return carry

    lax.fori_loop(1, ny * nz, wait_src, 0)

    def gram_block(k, carry):
        idx = (k + 5 * (1 - c)) % 10
        a = (idx + 4) // 8 + (idx + 1) // 8 + (idx + 1) // 10
        b = idx - (a * 4 - a * (a - 1) // 2) + a
        xa = xb[pl.ds(pl.multiple_of(a * BLK, BLK), BLK), :]
        xc = xb[pl.ds(pl.multiple_of(b * BLK, BLK), BLK), :]
        o = lax.dot_general(xa, xc, (((1,), (1,)), ((), ())), preferred_element_type=jnp.float32)
        gp[pl.ds(pl.multiple_of(idx * BLK, BLK), BLK), :] = o * scale
        return carry

    lax.fori_loop(0, 5, gram_block, 0)
    own = pl.multiple_of(c * half, 8)
    other = pl.multiple_of((1 - c) * half, 8)
    core_cp = pltpu.make_async_remote_copy(gp.at[pl.ds(other, half), :], rc, sc_sem.at[0], rc_sem.at[0],
                                           device_id=dev_id(x * 2 + 1 - c, d), device_id_type=MESH)
    core_cp.start()
    lax.fori_loop(5, 10, gram_block, 0)
    core_cp.wait_recv()
    hb[...] = gp[pl.ds(own, half), :] + rc[...]

    xy_cps = []
    for kx in range(nx):
        for ky in range(ny):
            if kx == 0 and ky == 0:
                continue
            px, py = (x + kx) % nx, (y + ky) % ny
            q = px * ny + py
            cp = pltpu.make_async_remote_copy(hb.at[pl.ds(pl.multiple_of(q * rows, 8), rows), :], rx.at[q_own],
                                              sx_sem.at[0, kx * ny + ky], rx_sem.at[0, q_own],
                                              device_id=dev_id(px * 2 + c, py * nz + z), device_id_type=MESH)
            cp.start()
            xy_cps.append(cp)
    rx[q_own] = hb[pl.ds(pl.multiple_of(q_own * rows, 8), rows), :]

    def wait_xy(k, carry):
        q = (q_own + k) % nq
        pltpu.make_async_copy(rx.at[q], rx.at[q], rx_sem.at[0, q]).wait()
        return carry

    lax.fori_loop(1, nq, wait_xy, 0)
    acc = rx[0]
    for q in range(1, nq):
        acc += rx[q]
    zb[...] = acc

    z_cps = []
    for kz in range(1, nz):
        pz = (z + kz) % nz
        cp = pltpu.make_async_remote_copy(zb, rz.at[z], sz_sem.at[kz], rz_sem.at[z],
                                          device_id=dev_id(g, y * nz + pz), device_id_type=MESH)
        cp.start()
        z_cps.append(cp)
    rz[z] = acc
    for kz in range(1, nz):
        pz = (z + kz) % nz
        pltpu.make_async_copy(rz.at[pz], rz.at[pz], rz_sem.at[pz]).wait()
    acc = rz[0]
    for k in range(1, nz):
        acc += rz[k]

    here = pl.ds(pl.multiple_of(own + q_own * rows, 8), rows)
    gf[here, :] = acc
    ag_cps = []
    for kx in range(nx):
        for ky in range(ny):
            if kx == 0 and ky == 0:
                continue
            px, py = (x + kx) % nx, (y + ky) % ny
            cp = pltpu.make_async_remote_copy(gf.at[here, :], gf.at[here, :],
                                              sx_sem.at[1, kx * ny + ky], rx_sem.at[1, q_own],
                                              device_id=dev_id(px * 2 + c, py * nz + z), device_id_type=MESH)
            cp.start()
            ag_cps.append(cp)

    def wait_ag(k, carry):
        q = (q_own + k) % nq
        r = gf.at[pl.ds(pl.multiple_of(own + q * rows, 8), rows), :]
        pltpu.make_async_copy(r, r, rx_sem.at[1, q]).wait()
        return carry

    lax.fori_loop(1, nq, wait_ag, 0)
    mine_half = gf.at[pl.ds(own, half), :]
    fin = pltpu.make_async_remote_copy(mine_half, mine_half, sg_sem.at[0], rg_sem.at[0],
                                       device_id=dev_id(x * 2 + 1 - c, d), device_id_type=MESH)
    fin.start()
    oth = gf.at[pl.ds(other, half), :]
    pltpu.make_async_copy(oth, oth, rg_sem.at[0]).wait()
    idx = 0
    for a in range(4):
        for b in range(a, 4):
            out_ref[b * BLK:(b + 1) * BLK, a * BLK:(a + 1) * BLK] = gf[idx * BLK:(idx + 1) * BLK, :].T
            if a != b:
                out_ref[a * BLK:(a + 1) * BLK, b * BLK:(b + 1) * BLK] = jnp.zeros((BLK, BLK), jnp.float32)
            idx += 1
    fin.wait_send()
    core_cp.wait_send()
    for cp in sends + xy_cps + z_cps + ag_cps:
        cp.wait_send()


def gram_total(tt, ft, nx, ny, nz, scale):
    jl, ks, ni = tt.shape
    n2 = jl * ny * nz
    nq = nx * ny
    half = 5 * BLK
    rows = half // nq
    cfg = (nx, ny, nz, jl, scale)
    f32, bf16 = jnp.float32, jnp.bfloat16
    dma = pltpu.SemaphoreType.DMA
    return pl.pallas_call(
        functools.partial(gram_body, cfg),
        out_shape=jax.ShapeDtypeStruct((n2, n2), f32),
        in_specs=[pl.BlockSpec(memory_space=pl.ANY), pl.BlockSpec(memory_space=pltpu.VMEM)],
        out_specs=pl.BlockSpec(memory_space=pltpu.VMEM),
        scratch_shapes=[
            pltpu.VMEM((ny, jl, BLK, ni), bf16),
            pltpu.VMEM((nz * jl * 8, BLK), f32),
            pltpu.VMEM((ny, nz, jl, 8 * BLK), bf16),
            pltpu.VMEM((n2, 8 * BLK), bf16),
            pltpu.VMEM((2 * half, BLK), f32),
            pltpu.VMEM((half, BLK), f32),
            pltpu.VMEM((half, BLK), f32),
            pltpu.VMEM((nq, rows, BLK), f32),
            pltpu.VMEM((rows, BLK), f32),
            pltpu.VMEM((nz, rows, BLK), f32),
            pltpu.VMEM((2 * half, BLK), f32),
            dma((ny,)),
            dma((ny, nz)), dma((ny * nz,)),
            dma((1,)), dma((1,)),
            dma((2, nq)), dma((2, nq)),
            dma((nz,)), dma((nz,)),
            dma((1,)), dma((1,)),
        ],
        compiler_params=pltpu.CompilerParams(collective_id=0, has_side_effects=True, vmem_limit_bytes=48 << 20),
    )(tt, ft)


def own_block(full_tri):
    order = full_tri.shape[0]
    row_count = order // lax.axis_size("dev")
    col_count = order // lax.axis_size("grp")
    row_start = lax.axis_index("dev") * row_count
    col_start = lax.axis_index("grp") * col_count
    return lax.dynamic_slice(full_tri, (row_start, col_start), (row_count, col_count))


def per_device(ny, tensor_slab, mode_factor):
    ni, jl, kl, s = tensor_slab.shape
    grp, dev = lax.axis_size("grp"), lax.axis_size("dev")
    tt = jnp.transpose(tensor_slab, (1, 2, 3, 0)).reshape(jl, kl * s, ni)
    row_total = mode_factor.shape[1] * kl * s * grp
    gram = gram_total(tt, mode_factor.T, grp // 2, ny, dev // ny, 1.0 / row_total)
    return own_block(jnp.linalg.cholesky(gram, symmetrize_input=False).T)


def solution(mesh, ny=NY):
    in_specs = (P(None, "dev", "grp", None), P())
    out_specs = P("dev", "grp")
    return jax.shard_map(
        functools.partial(per_device, ny), mesh=mesh, in_specs=in_specs, out_specs=out_specs, check_vma=False
    )
```

```python
import functools

import jax
import jax.numpy as jnp
from jax import lax
from jax.experimental import pallas as pl
from jax.experimental.pallas import tpu as pltpu
from jax.sharding import PartitionSpec as P

MESH = pl.DeviceIdType.MESH
BLK = 128
NY = 4
SUB = 16


def split3(v):
    hi = v.astype(jnp.bfloat16)
    rest = v - hi.astype(jnp.float32)
    mid = rest.astype(jnp.bfloat16)
    low = (rest - mid.astype(jnp.float32)).astype(jnp.bfloat16)
    return hi, mid, low


def gram_like(a, b):
    ah, am, al = split3(a)
    bh, bm, bl = split3(b)
    lhs = jnp.concatenate([ah, ah, am, ah, am, al], axis=0)
    rhs = jnp.concatenate([bh, bm, bh, bl, bm, bh], axis=0)
    return lax.dot_general(lhs, rhs, (((0,), (0,)), ((), ())), preferred_element_type=jnp.float32)


def spread(v, q):
    return jnp.broadcast_to(v[q:q + 1, :], (8, BLK))


def factor_rows(rows, left):
    sub = lax.broadcasted_iota(jnp.int32, (8, BLK), 0)
    low, high = [], []
    for q in range(SUB):
        lane = left + q
        low.append(jnp.broadcast_to(rows[0][0][:, lane:lane + 1], (8, BLK)) if q < 8 else None)
        high.append(jnp.broadcast_to(rows[0][1][:, lane:lane + 1], (8, BLK)))
    rows = [list(r) for r in rows]
    piv = [jnp.ones((8, BLK), jnp.float32)] * 2

    def at(q, p):
        return spread(low[q], p) if p < 8 else spread(high[q], p - 8)

    d = at(0, 0)
    for q in range(SUB):
        r = 1.0 / d
        piv[q // 8] = jnp.where(sub == q % 8, d, piv[q // 8])
        if q == SUB - 1:
            break
        e = at(q, q + 1)
        d = at(q + 1, q + 1) - (e * e) * r
        m_low = low[q] * r if q < 7 else None
        m_high = high[q] * r
        for p in range(q + 1, SUB):
            e = at(q, p)
            if p < 8:
                low[p] = low[p] - m_low * e
            high[p] = high[p] - m_high * e
        k_low = jnp.where(sub > q, m_low, 0.0) if q < 7 else None
        k_high = m_high if q < 8 else jnp.where(sub > q - 8, m_high, 0.0)
        for t in rows:
            e = spread(t[q // 8], q % 8)
            if q < 7:
                t[0] = t[0] - k_low * e
            t[1] = t[1] - k_high * e
    s0, s1 = lax.rsqrt(piv[0]), lax.rsqrt(piv[1])
    return [jnp.concatenate([t[0] * s0, t[1] * s1], axis=0) for t in rows]


def block_at(a, b):
    return a * 4 - a * (a - 1) // 2 + b - a


def cholesky_packed(g, inv):
    n = 4
    for k in range(n):
        base = block_at(k, k) * BLK
        last = k == n - 1
        if not last:
            inv[...] = (lax.broadcasted_iota(jnp.int32, (BLK, BLK), 0) == lax.broadcasted_iota(jnp.int32, (BLK, BLK), 1)).astype(jnp.float32)
        refs = [(g, base)] if last else [(g, base), (inv, 0)]
        for s in range(BLK // SUB):
            at = s * SUB
            tiles = [(r[o + at:o + at + 8, :], r[o + at + 8:o + at + SUB, :]) for r, o in refs]
            done = factor_rows(tiles, at)
            for (r, o), v in zip(refs, done):
                r[o + at:o + at + SUB, :] = v
            end = at + SUB
            if end < BLK:
                both = done[0] if last else jnp.concatenate(done, axis=1)
                upd = gram_like(done[0], both)
                for i, (r, o) in enumerate(refs):
                    r[o + end:o + BLK, :] = r[o + end:o + BLK, :] - upd[end:, i * BLK:(i + 1) * BLK]
        if last:
            break
        row = []
        for b in range(k + 1, n):
            o = block_at(k, b) * BLK
            u = lax.dot_general(inv[...], g[o:o + BLK, :], (((1,), (0,)), ((), ())), precision=lax.Precision.HIGHEST, preferred_element_type=jnp.float32)
            g[o:o + BLK, :] = u
            row.append(u)
        for a in range(k + 1, n):
            for b in range(a, n):
                o = block_at(a, b) * BLK
                g[o:o + BLK, :] = g[o:o + BLK, :] - gram_like(row[a - k - 1], row[b - k - 1])


def own_part(g, row, col):
    a, b = row // 8, col // 2
    o = pl.multiple_of(block_at(a, b) * BLK + (row % 8) * 16, 16)
    v = g[pl.ds(o, 16), :]
    shifted = jnp.concatenate([v[:, 64:], v[:, :64]], axis=1)
    i = row * 16 + lax.broadcasted_iota(jnp.int32, (16, BLK), 0)
    j = col * 64 + lax.broadcasted_iota(jnp.int32, (16, BLK), 1)
    half = lax.broadcasted_iota(jnp.int32, (16, BLK), 1) * 0 + col % 2
    v = jnp.where(half == 1, shifted, v)
    return jnp.where(j >= i, v, 0.0)[:, :64]


def gram_body(cfg, tt_ref, ft_ref, out_ref, tb, pf, sb, xb, gp, rc, hb, rx, zb, rz, gf, inv,
              ld_sem, sa_sem, ra_sem, sc_sem, rc_sem, sx_sem, rx_sem, sz_sem, rz_sem, sg_sem, rg_sem):
    nx, ny, nz, jl, scale = cfg
    half = gp.shape[0] // 2
    nq = nx * ny
    rows = half // nq
    g = lax.axis_index("grp")
    d = lax.axis_index("dev")
    x, c = g // 2, g % 2
    y, z = d // nz, d % nz
    q_own = x * ny + y

    def dev_id(gg, dd):
        return {"grp": gg, "dev": dd}

    chunks = []
    for t in range(ny):
        cg = (y + 1 + t) % ny
        cp = pltpu.make_async_copy(tt_ref.at[:, pl.ds(pl.multiple_of(cg * BLK, BLK), BLK), :], tb.at[t], ld_sem.at[t])
        cp.start()
        chunks.append(cp)

    barrier = pltpu.get_barrier_semaphore()
    nbar = 0

    def sig(gg, dd):
        pl.semaphore_signal(barrier, inc=1, device_id=dev_id(gg, dd), device_id_type=MESH)

    for k in range(1, ny * nz):
        sig(g, (d + k) % (ny * nz))
        nbar += 1
    for kx in range(1, nx):
        for ky in range(ny):
            sig(((x + kx) % nx) * 2 + c, ((y + ky) % ny) * nz + z)
            nbar += 1
    sig(x * 2 + 1 - c, d)
    nbar += 1

    zorder = sorted(range(nz), key=lambda k: (-min(k, nz - k), k))
    mine = pl.ds(pl.multiple_of(d * jl, jl), jl)
    jg = 256 // BLK
    sends = []
    for t in range(ny):
        chunks[t].wait()

        def proj(i, carry):
            rhs = tb[t, pl.ds(i * jg, jg)].reshape(jg * BLK, tb.shape[-1])
            o = lax.dot_general(ft_ref[...], rhs, (((1,), (1,)), ((), ())), preferred_element_type=jnp.float32)
            for rg in range(nz):
                for jj in range(jg):
                    pf[pl.ds(pl.multiple_of(rg * jl * 8 + (i * jg + jj) * 8, 8), 8), :] = o[rg * 8:(rg + 1) * 8, jj * BLK:(jj + 1) * BLK]
            return carry

        lax.fori_loop(0, jl // jg, proj, 0)
        cg = (y + 1 + t) % ny
        for n, zo in enumerate(zorder):
            rg = (z + zo) % nz
            local = t == ny - 1 and zo == 0
            for r in range(8):
                v = pf[pl.ds(pl.multiple_of(rg * jl * 8, 8) + r, jl, stride=8), :].astype(jnp.bfloat16)
                if local:
                    xb[mine, r * BLK:(r + 1) * BLK] = v
                else:
                    sb[t, n, :, r * BLK:(r + 1) * BLK] = v
            if t == 0 and n == 0:
                pl.semaphore_wait(barrier, nbar)
            if not local:
                cp = pltpu.make_async_remote_copy(sb.at[t, n], xb.at[mine, :], sa_sem.at[t, n], ra_sem.at[d],
                                                  device_id=dev_id(g, cg * nz + rg), device_id_type=MESH)
                cp.start()
                sends.append(cp)

    def wait_src(k, carry):
        src = (d + k) % (ny * nz)
        blk = xb.at[pl.ds(pl.multiple_of(src * jl, jl), jl), :]
        pltpu.make_async_copy(blk, blk, ra_sem.at[src]).wait()
        return carry

    lax.fori_loop(1, ny * nz, wait_src, 0)

    def gram_block(k, carry):
        idx = (k + 5 * (1 - c)) % 10
        a = (idx + 4) // 8 + (idx + 1) // 8 + (idx + 1) // 10
        b = idx - (a * 4 - a * (a - 1) // 2) + a
        xa = xb[pl.ds(pl.multiple_of(a * BLK, BLK), BLK), :]
        xc = xb[pl.ds(pl.multiple_of(b * BLK, BLK), BLK), :]
        o = lax.dot_general(xa, xc, (((1,), (1,)), ((), ())), preferred_element_type=jnp.float32)
        gp[pl.ds(pl.multiple_of(idx * BLK, BLK), BLK), :] = o * scale
        return carry

    lax.fori_loop(0, 5, gram_block, 0)
    own = pl.multiple_of(c * half, 8)
    other = pl.multiple_of((1 - c) * half, 8)
    core_cp = pltpu.make_async_remote_copy(gp.at[pl.ds(other, half), :], rc, sc_sem.at[0], rc_sem.at[0],
                                           device_id=dev_id(x * 2 + 1 - c, d), device_id_type=MESH)
    core_cp.start()
    lax.fori_loop(5, 10, gram_block, 0)
    core_cp.wait_recv()
    hb[...] = gp[pl.ds(own, half), :] + rc[...]

    xy_cps = []
    for kx in range(nx):
        for ky in range(ny):
            if kx == 0 and ky == 0:
                continue
            px, py = (x + kx) % nx, (y + ky) % ny
            q = px * ny + py
            cp = pltpu.make_async_remote_copy(hb.at[pl.ds(pl.multiple_of(q * rows, 8), rows), :], rx.at[q_own],
                                              sx_sem.at[0, kx * ny + ky], rx_sem.at[0, q_own],
                                              device_id=dev_id(px * 2 + c, py * nz + z), device_id_type=MESH)
            cp.start()
            xy_cps.append(cp)
    rx[q_own] = hb[pl.ds(pl.multiple_of(q_own * rows, 8), rows), :]

    def wait_xy(k, carry):
        q = (q_own + k) % nq
        pltpu.make_async_copy(rx.at[q], rx.at[q], rx_sem.at[0, q]).wait()
        return carry

    lax.fori_loop(1, nq, wait_xy, 0)
    acc = rx[0]
    for q in range(1, nq):
        acc += rx[q]
    zb[...] = acc

    z_cps = []
    for kz in range(1, nz):
        pz = (z + kz) % nz
        cp = pltpu.make_async_remote_copy(zb, rz.at[z], sz_sem.at[kz], rz_sem.at[z],
                                          device_id=dev_id(g, y * nz + pz), device_id_type=MESH)
        cp.start()
        z_cps.append(cp)
    rz[z] = acc
    for kz in range(1, nz):
        pz = (z + kz) % nz
        pltpu.make_async_copy(rz.at[pz], rz.at[pz], rz_sem.at[pz]).wait()
    acc = rz[0]
    for k in range(1, nz):
        acc += rz[k]

    here = pl.ds(pl.multiple_of(own + q_own * rows, 8), rows)
    gf[here, :] = acc
    ag_cps = []
    for kx in range(nx):
        for ky in range(ny):
            if kx == 0 and ky == 0:
                continue
            px, py = (x + kx) % nx, (y + ky) % ny
            cp = pltpu.make_async_remote_copy(gf.at[here, :], gf.at[here, :],
                                              sx_sem.at[1, kx * ny + ky], rx_sem.at[1, q_own],
                                              device_id=dev_id(px * 2 + c, py * nz + z), device_id_type=MESH)
            cp.start()
            ag_cps.append(cp)

    def wait_ag(k, carry):
        q = (q_own + k) % nq
        r = gf.at[pl.ds(pl.multiple_of(own + q * rows, 8), rows), :]
        pltpu.make_async_copy(r, r, rx_sem.at[1, q]).wait()
        return carry

    lax.fori_loop(1, nq, wait_ag, 0)
    mine_half = gf.at[pl.ds(own, half), :]
    fin = pltpu.make_async_remote_copy(mine_half, mine_half, sg_sem.at[0], rg_sem.at[0],
                                       device_id=dev_id(x * 2 + 1 - c, d), device_id_type=MESH)
    fin.start()
    oth = gf.at[pl.ds(other, half), :]
    pltpu.make_async_copy(oth, oth, rg_sem.at[0]).wait()
    fin.wait_send()
    core_cp.wait_send()
    for cp in sends + xy_cps + z_cps + ag_cps:
        cp.wait_send()
    cholesky_packed(gf, inv)
    out_ref[...] = own_part(gf, d, g)


def triangle(tt, ft, nx, ny, nz, scale):
    jl, ks, ni = tt.shape
    n2 = jl * ny * nz
    nq = nx * ny
    half = 5 * BLK
    rows = half // nq
    cfg = (nx, ny, nz, jl, scale)
    f32, bf16 = jnp.float32, jnp.bfloat16
    dma = pltpu.SemaphoreType.DMA
    return pl.pallas_call(
        functools.partial(gram_body, cfg),
        out_shape=jax.ShapeDtypeStruct((n2 // (ny * nz), n2 // (2 * nx)), f32),
        in_specs=[pl.BlockSpec(memory_space=pl.ANY), pl.BlockSpec(memory_space=pltpu.VMEM)],
        out_specs=pl.BlockSpec(memory_space=pltpu.VMEM),
        scratch_shapes=[
            pltpu.VMEM((ny, jl, BLK, ni), bf16),
            pltpu.VMEM((nz * jl * 8, BLK), f32),
            pltpu.VMEM((ny, nz, jl, 8 * BLK), bf16),
            pltpu.VMEM((n2, 8 * BLK), bf16),
            pltpu.VMEM((2 * half, BLK), f32),
            pltpu.VMEM((half, BLK), f32),
            pltpu.VMEM((half, BLK), f32),
            pltpu.VMEM((nq, rows, BLK), f32),
            pltpu.VMEM((rows, BLK), f32),
            pltpu.VMEM((nz, rows, BLK), f32),
            pltpu.VMEM((2 * half, BLK), f32),
            pltpu.VMEM((BLK, BLK), f32),
            dma((ny,)),
            dma((ny, nz)), dma((ny * nz,)),
            dma((1,)), dma((1,)),
            dma((2, nq)), dma((2, nq)),
            dma((nz,)), dma((nz,)),
            dma((1,)), dma((1,)),
        ],
        compiler_params=pltpu.CompilerParams(collective_id=0, has_side_effects=True, vmem_limit_bytes=48 << 20),
    )(tt, ft)


def per_device(ny, tensor_slab, mode_factor):
    ni, jl, kl, s = tensor_slab.shape
    grp, dev = lax.axis_size("grp"), lax.axis_size("dev")
    tt = jnp.transpose(tensor_slab, (1, 2, 3, 0)).reshape(jl, kl * s, ni)
    row_total = mode_factor.shape[1] * kl * s * grp
    return triangle(tt, mode_factor.T, grp // 2, ny, dev // ny, 1.0 / row_total)


def solution(mesh, ny=NY):
    in_specs = (P(None, "dev", "grp", None), P())
    out_specs = P("dev", "grp")
    return jax.shard_map(
        functools.partial(per_device, ny), mesh=mesh, in_specs=in_specs, out_specs=out_specs, check_vma=False
    )
```

```python
import functools

import jax
import jax.numpy as jnp
from jax import lax
from jax.experimental import pallas as pl
from jax.experimental.pallas import tpu as pltpu
from jax.sharding import PartitionSpec as P

MESH = pl.DeviceIdType.MESH
BLK = 128
NY = 4
SUB = 16
STRIP = 32


def split3(v):
    hi = v.astype(jnp.bfloat16)
    rest = v - hi.astype(jnp.float32)
    mid = rest.astype(jnp.bfloat16)
    low = (rest - mid.astype(jnp.float32)).astype(jnp.bfloat16)
    return hi, mid, low


def gram_like(a, b):
    ah, am, al = split3(a)
    bh, bm, bl = split3(b)
    lhs = jnp.concatenate([ah, ah, am, ah, am, al], axis=0)
    rhs = jnp.concatenate([bh, bm, bh, bl, bm, bh], axis=0)
    return lax.dot_general(lhs, rhs, (((0,), (0,)), ((), ())), preferred_element_type=jnp.float32)


def spread(v, q):
    return jnp.broadcast_to(v[q:q + 1, :], (8, BLK))


def eliminate(rows, left, first):
    sub = lax.broadcasted_iota(jnp.int32, (8, BLK), 0)
    pieces = range(first, len(rows[0]))
    col = [{i: jnp.broadcast_to(rows[0][i][:, left + q:left + q + 1], (8, BLK)) for i in pieces if i > first or q < 8}
           for q in range(SUB)]
    piv = [jnp.ones((8, BLK), jnp.float32)] * 2

    def at(q, p):
        return spread(col[q][first + p // 8], p % 8)

    d = at(0, 0)
    for q in range(SUB):
        r = 1.0 / d
        piv[q // 8] = jnp.where(sub == q % 8, d, piv[q // 8])
        if q < SUB - 1:
            e = at(q, q + 1)
            d = at(q + 1, q + 1) - (e * e) * r
        mult = {i: v * r for i, v in col[q].items() if i >= first + q // 8}
        for p in range(q + 1, SUB):
            e = at(q, p)
            for i in col[p]:
                if i >= first + p // 8:
                    col[p][i] = col[p][i] - mult[i] * e
        here = first + q // 8
        for t in rows:
            e = spread(t[here], q % 8)
            for i in mult:
                if i > here:
                    t[i] = t[i] - mult[i] * e
                elif q % 8 < 7:
                    t[i] = t[i] - jnp.where(sub > q % 8, mult[i], 0.0) * e
    return [lax.rsqrt(v) for v in piv]


def factor_rows(rows, left):
    rows = [list(t) for t in rows]
    scales = []
    for first in range(0, len(rows[0]), 2):
        scales += eliminate(rows, left + first * 8, first)
    return [jnp.concatenate([v * s for v, s in zip(t, scales)], axis=0) for t in rows]


def block_at(a, b):
    return a * 4 - a * (a - 1) // 2 + b - a


def cholesky_packed(g, inv):
    n = 4
    for k in range(n):
        base = block_at(k, k) * BLK
        last = k == n - 1
        if not last:
            inv[...] = (lax.broadcasted_iota(jnp.int32, (BLK, BLK), 0) == lax.broadcasted_iota(jnp.int32, (BLK, BLK), 1)).astype(jnp.float32)
        refs = [(g, base)] if last else [(g, base), (inv, 0)]
        for s in range(BLK // STRIP):
            at = s * STRIP
            tiles = [[r[o + at + i:o + at + i + 8, :] for i in range(0, STRIP, 8)] for r, o in refs]
            done = factor_rows(tiles, at)
            for (r, o), v in zip(refs, done):
                r[o + at:o + at + STRIP, :] = v
            end = at + STRIP
            if end < BLK:
                both = done[0] if last else jnp.concatenate(done, axis=1)
                upd = gram_like(done[0], both)
                for i, (r, o) in enumerate(refs):
                    r[o + end:o + BLK, :] = r[o + end:o + BLK, :] - upd[end:, i * BLK:(i + 1) * BLK]
        if last:
            break
        row = []
        for b in range(k + 1, n):
            o = block_at(k, b) * BLK
            u = lax.dot_general(inv[...], g[o:o + BLK, :], (((1,), (0,)), ((), ())), precision=lax.Precision.HIGHEST, preferred_element_type=jnp.float32)
            g[o:o + BLK, :] = u
            row.append(u)
        for a in range(k + 1, n):
            for b in range(a, n):
                o = block_at(a, b) * BLK
                g[o:o + BLK, :] = g[o:o + BLK, :] - gram_like(row[a - k - 1], row[b - k - 1])


def own_part(g, row, col):
    a, b = row // 8, col // 2
    o = pl.multiple_of(block_at(a, b) * BLK + (row % 8) * 16, 16)
    v = g[pl.ds(o, 16), :]
    shifted = jnp.concatenate([v[:, 64:], v[:, :64]], axis=1)
    i = row * 16 + lax.broadcasted_iota(jnp.int32, (16, BLK), 0)
    j = col * 64 + lax.broadcasted_iota(jnp.int32, (16, BLK), 1)
    half = lax.broadcasted_iota(jnp.int32, (16, BLK), 1) * 0 + col % 2
    v = jnp.where(half == 1, shifted, v)
    return jnp.where(j >= i, v, 0.0)[:, :64]


def gram_body(cfg, tt_ref, ft_any, out_ref, ft_ref, tb, pf, sb, xb, gp, rc, hb, rx, zb, rz, gf, inv,
              ld_sem, sa_sem, ra_sem, sc_sem, rc_sem, sx_sem, rx_sem, sz_sem, rz_sem, sg_sem, rg_sem, ft_sem):
    nx, ny, nz, jl, scale = cfg
    half = gp.shape[0] // 2
    nq = nx * ny
    rows = half // nq
    g = lax.axis_index("grp")
    d = lax.axis_index("dev")
    x, c = g // 2, g % 2
    y, z = d // nz, d % nz
    q_own = x * ny + y

    def dev_id(gg, dd):
        return {"grp": gg, "dev": dd}

    ft_cp = pltpu.make_async_copy(ft_any, ft_ref, ft_sem)
    ft_cp.start()
    chunks = []
    for t in range(ny):
        cg = (y + 1 + t) % ny
        cp = pltpu.make_async_copy(tt_ref.at[:, pl.ds(pl.multiple_of(cg * BLK, BLK), BLK), :], tb.at[t], ld_sem.at[t])
        cp.start()
        chunks.append(cp)

    barrier = pltpu.get_barrier_semaphore()
    nbar = 0

    def sig(gg, dd):
        pl.semaphore_signal(barrier, inc=1, device_id=dev_id(gg, dd), device_id_type=MESH)

    for k in range(1, ny * nz):
        sig(g, (d + k) % (ny * nz))
        nbar += 1
    for kx in range(1, nx):
        for ky in range(ny):
            sig(((x + kx) % nx) * 2 + c, ((y + ky) % ny) * nz + z)
            nbar += 1
    sig(x * 2 + 1 - c, d)
    nbar += 1

    zorder = sorted(range(nz), key=lambda k: (-min(k, nz - k), k))
    mine = pl.ds(pl.multiple_of(d * jl, jl), jl)
    jg = 256 // BLK
    sends = []
    ft_cp.wait()
    for t in range(ny):
        chunks[t].wait()

        def proj(i, carry):
            rhs = tb[t, pl.ds(i * jg, jg)].reshape(jg * BLK, tb.shape[-1])
            o = lax.dot_general(ft_ref[...], rhs, (((1,), (1,)), ((), ())), preferred_element_type=jnp.float32)
            for rg in range(nz):
                for jj in range(jg):
                    pf[pl.ds(pl.multiple_of(rg * jl * 8 + (i * jg + jj) * 8, 8), 8), :] = o[rg * 8:(rg + 1) * 8, jj * BLK:(jj + 1) * BLK]
            return carry

        lax.fori_loop(0, jl // jg, proj, 0)
        cg = (y + 1 + t) % ny
        for n, zo in enumerate(zorder):
            rg = (z + zo) % nz
            local = t == ny - 1 and zo == 0
            for r in range(8):
                v = pf[pl.ds(pl.multiple_of(rg * jl * 8, 8) + r, jl, stride=8), :].astype(jnp.bfloat16)
                if local:
                    xb[mine, r * BLK:(r + 1) * BLK] = v
                else:
                    sb[t, n, :, r * BLK:(r + 1) * BLK] = v
            if t == 0 and n == 0:
                pl.semaphore_wait(barrier, nbar)
            if not local:
                cp = pltpu.make_async_remote_copy(sb.at[t, n], xb.at[mine, :], sa_sem.at[t, n], ra_sem.at[d],
                                                  device_id=dev_id(g, cg * nz + rg), device_id_type=MESH)
                cp.start()
                sends.append(cp)

    def wait_src(k, carry):
        src = (d + k) % (ny * nz)
        blk = xb.at[pl.ds(pl.multiple_of(src * jl, jl), jl), :]
        pltpu.make_async_copy(blk, blk, ra_sem.at[src]).wait()
        return carry

    lax.fori_loop(1, ny * nz, wait_src, 0)

    def gram_block(k, carry):
        idx = (k + 5 * (1 - c)) % 10
        a = (idx + 4) // 8 + (idx + 1) // 8 + (idx + 1) // 10
        b = idx - (a * 4 - a * (a - 1) // 2) + a
        xa = xb[pl.ds(pl.multiple_of(a * BLK, BLK), BLK), :]
        xc = xb[pl.ds(pl.multiple_of(b * BLK, BLK), BLK), :]
        o = lax.dot_general(xa, xc, (((1,), (1,)), ((), ())), preferred_element_type=jnp.float32)
        gp[pl.ds(pl.multiple_of(idx * BLK, BLK), BLK), :] = o * scale
        return carry

    lax.fori_loop(0, 5, gram_block, 0)
    own = pl.multiple_of(c * half, 8)
    other = pl.multiple_of((1 - c) * half, 8)
    core_cp = pltpu.make_async_remote_copy(gp.at[pl.ds(other, half), :], rc, sc_sem.at[0], rc_sem.at[0],
                                           device_id=dev_id(x * 2 + 1 - c, d), device_id_type=MESH)
    core_cp.start()
    lax.fori_loop(5, 10, gram_block, 0)
    core_cp.wait_recv()
    hb[...] = gp[pl.ds(own, half), :] + rc[...]

    plane = sorted(((kx, ky) for kx in range(nx) for ky in range(ny)), key=lambda k: min(k[0], nx - k[0]) + min(k[1], ny - k[1]))
    xy_cps = []
    for kx in range(nx):
        for ky in range(ny):
            if kx == 0 and ky == 0:
                continue
            px, py = (x + kx) % nx, (y + ky) % ny
            q = px * ny + py
            cp = pltpu.make_async_remote_copy(hb.at[pl.ds(pl.multiple_of(q * rows, 8), rows), :], rx.at[q_own],
                                              sx_sem.at[0, kx * ny + ky], rx_sem.at[0, q_own],
                                              device_id=dev_id(px * 2 + c, py * nz + z), device_id_type=MESH)
            cp.start()
            xy_cps.append(cp)
    rx[q_own] = hb[pl.ds(pl.multiple_of(q_own * rows, 8), rows), :]

    def wait_xy(k, carry):
        q = (q_own + k) % nq
        pltpu.make_async_copy(rx.at[q], rx.at[q], rx_sem.at[0, q]).wait()
        return carry

    lax.fori_loop(1, nq, wait_xy, 0)
    acc = rx[0]
    for q in range(1, nq):
        acc += rx[q]
    zb[...] = acc

    z_cps = []
    for kz in range(1, nz):
        pz = (z + kz) % nz
        cp = pltpu.make_async_remote_copy(zb, rz.at[z], sz_sem.at[kz], rz_sem.at[z],
                                          device_id=dev_id(g, y * nz + pz), device_id_type=MESH)
        cp.start()
        z_cps.append(cp)
    rz[z] = acc
    for kz in range(1, nz):
        pz = (z + kz) % nz
        pltpu.make_async_copy(rz.at[pz], rz.at[pz], rz_sem.at[pz]).wait()
    acc = rz[0]
    for k in range(1, nz):
        acc += rz[k]

    here = pl.ds(pl.multiple_of(own + q_own * rows, 8), rows)
    gf[here, :] = acc
    ag_cps = []
    for kx in range(nx):
        for ky in range(ny):
            if kx == 0 and ky == 0:
                continue
            px, py = (x + kx) % nx, (y + ky) % ny
            cp = pltpu.make_async_remote_copy(gf.at[here, :], gf.at[here, :],
                                              sx_sem.at[1, kx * ny + ky], rx_sem.at[1, q_own],
                                              device_id=dev_id(px * 2 + c, py * nz + z), device_id_type=MESH)
            cp.start()
            ag_cps.append(cp)

    forward = []
    for kx, ky in plane:
        q = ((x + kx) % nx) * ny + (y + ky) % ny
        piece = gf.at[pl.ds(pl.multiple_of(own + q * rows, 8), rows), :]
        if (kx, ky) != (0, 0):
            pltpu.make_async_copy(piece, piece, rx_sem.at[1, q]).wait()
        cp = pltpu.make_async_remote_copy(piece, piece, sg_sem.at[q], rg_sem.at[q],
                                          device_id=dev_id(x * 2 + 1 - c, d), device_id_type=MESH)
        cp.start()
        forward.append(cp)
    for q in range(nq):
        piece = gf.at[pl.ds(pl.multiple_of(other + q * rows, 8), rows), :]
        pltpu.make_async_copy(piece, piece, rg_sem.at[q]).wait()
    core_cp.wait_send()
    for cp in sends + xy_cps + z_cps + ag_cps + forward:
        cp.wait_send()
    cholesky_packed(gf, inv)
    out_ref[...] = own_part(gf, d, g)


def triangle(tt, ft, nx, ny, nz, scale):
    jl, ks, ni = tt.shape
    n2 = jl * ny * nz
    nq = nx * ny
    half = 5 * BLK
    rows = half // nq
    cfg = (nx, ny, nz, jl, scale)
    f32, bf16 = jnp.float32, jnp.bfloat16
    dma = pltpu.SemaphoreType.DMA
    return pl.pallas_call(
        functools.partial(gram_body, cfg),
        out_shape=jax.ShapeDtypeStruct((n2 // (ny * nz), n2 // (2 * nx)), f32),
        in_specs=[pl.BlockSpec(memory_space=pl.ANY)] * 2,
        out_specs=pl.BlockSpec(memory_space=pltpu.VMEM),
        scratch_shapes=[
            pltpu.VMEM(ft.shape, bf16),
            pltpu.VMEM((ny, jl, BLK, ni), bf16),
            pltpu.VMEM((nz * jl * 8, BLK), f32),
            pltpu.VMEM((ny, nz, jl, 8 * BLK), bf16),
            pltpu.VMEM((n2, 8 * BLK), bf16),
            pltpu.VMEM((2 * half, BLK), f32),
            pltpu.VMEM((half, BLK), f32),
            pltpu.VMEM((half, BLK), f32),
            pltpu.VMEM((nq, rows, BLK), f32),
            pltpu.VMEM((rows, BLK), f32),
            pltpu.VMEM((nz, rows, BLK), f32),
            pltpu.VMEM((2 * half, BLK), f32),
            pltpu.VMEM((BLK, BLK), f32),
            dma((ny,)),
            dma((ny, nz)), dma((ny * nz,)),
            dma((1,)), dma((1,)),
            dma((2, nq)), dma((2, nq)),
            dma((nz,)), dma((nz,)),
            dma((nq,)), dma((nq,)),
            dma(()),
        ],
        compiler_params=pltpu.CompilerParams(collective_id=0, has_side_effects=True, vmem_limit_bytes=48 << 20),
    )(tt, ft)


def per_device(ny, tensor_slab, mode_factor):
    ni, jl, kl, s = tensor_slab.shape
    grp, dev = lax.axis_size("grp"), lax.axis_size("dev")
    tt = jnp.transpose(tensor_slab, (1, 2, 3, 0)).reshape(jl, kl * s, ni)
    row_total = mode_factor.shape[1] * kl * s * grp
    return triangle(tt, mode_factor.T, grp // 2, ny, dev // ny, 1.0 / row_total)


def solution(mesh, ny=NY):
    in_specs = (P(None, "dev", "grp", None), P())
    out_specs = P("dev", "grp")
    return jax.shard_map(
        functools.partial(per_device, ny), mesh=mesh, in_specs=in_specs, out_specs=out_specs, check_vma=False
    )
```

```python
import functools

import jax
import jax.numpy as jnp
from jax import lax
from jax.experimental import pallas as pl
from jax.experimental.pallas import tpu as pltpu
from jax.sharding import PartitionSpec as P

MESH = pl.DeviceIdType.MESH
BLK = 128
NY = 4
SUB = 16
STRIP = 32


def split3(v):
    hi = v.astype(jnp.bfloat16)
    rest = v - hi.astype(jnp.float32)
    mid = rest.astype(jnp.bfloat16)
    low = (rest - mid.astype(jnp.float32)).astype(jnp.bfloat16)
    return hi, mid, low


def gram_like(a, b):
    ah, am, al = split3(a)
    bh, bm, bl = split3(b)
    lhs = jnp.concatenate([ah, ah, am, ah, am, al], axis=0)
    rhs = jnp.concatenate([bh, bm, bh, bl, bm, bh], axis=0)
    return lax.dot_general(lhs, rhs, (((0,), (0,)), ((), ())), preferred_element_type=jnp.float32)


def spread(v, q):
    return jnp.broadcast_to(v[q:q + 1, :], (8, BLK))


def eliminate(rows, left, first):
    sub = lax.broadcasted_iota(jnp.int32, (8, BLK), 0)
    pieces = range(first, len(rows[0]))
    col = [{i: jnp.broadcast_to(rows[0][i][:, left + q:left + q + 1], (8, BLK)) for i in pieces if i > first or q < 8}
           for q in range(SUB)]
    piv = [jnp.ones((8, BLK), jnp.float32)] * 2

    def at(q, p):
        return spread(col[q][first + p // 8], p % 8)

    d = at(0, 0)
    for q in range(SUB):
        r = 1.0 / d
        piv[q // 8] = jnp.where(sub == q % 8, d, piv[q // 8])
        if q < SUB - 1:
            e = at(q, q + 1)
            d = at(q + 1, q + 1) - (e * e) * r
        mult = {i: v * r for i, v in col[q].items() if i >= first + q // 8}
        for p in range(q + 1, SUB):
            e = at(q, p)
            for i in col[p]:
                if i >= first + p // 8:
                    col[p][i] = col[p][i] - mult[i] * e
        here = first + q // 8
        for t in rows:
            e = spread(t[here], q % 8)
            for i in mult:
                if i > here:
                    t[i] = t[i] - mult[i] * e
                elif q % 8 < 7:
                    t[i] = t[i] - jnp.where(sub > q % 8, mult[i], 0.0) * e
    return [lax.rsqrt(v) for v in piv]


def factor_rows(rows, left):
    rows = [list(t) for t in rows]
    scales = []
    for first in range(0, len(rows[0]), 2):
        scales += eliminate(rows, left + first * 8, first)
    return [jnp.concatenate([v * s for v, s in zip(t, scales)], axis=0) for t in rows]


def block_at(a, b):
    return a * 4 - a * (a - 1) // 2 + b - a


def cholesky_packed(g, inv):
    n = 4
    for k in range(n):
        base = block_at(k, k) * BLK
        last = k == n - 1
        if not last:
            inv[...] = (lax.broadcasted_iota(jnp.int32, (BLK, BLK), 0) == lax.broadcasted_iota(jnp.int32, (BLK, BLK), 1)).astype(jnp.float32)
        refs = [(g, base)] if last else [(g, base), (inv, 0)]
        for s in range(BLK // STRIP):
            at = s * STRIP
            tiles = [[r[o + at + i:o + at + i + 8, :] for i in range(0, STRIP, 8)] for r, o in refs]
            done = factor_rows(tiles, at)
            for (r, o), v in zip(refs, done):
                r[o + at:o + at + STRIP, :] = v
            end = at + STRIP
            if end < BLK:
                both = done[0] if last else jnp.concatenate(done, axis=1)
                upd = gram_like(done[0], both)
                for i, (r, o) in enumerate(refs):
                    r[o + end:o + BLK, :] = r[o + end:o + BLK, :] - upd[end:, i * BLK:(i + 1) * BLK]
        if last:
            break
        row = []
        for b in range(k + 1, n):
            o = block_at(k, b) * BLK
            u = lax.dot_general(inv[...], g[o:o + BLK, :], (((1,), (0,)), ((), ())), precision=lax.Precision.HIGHEST, preferred_element_type=jnp.float32)
            g[o:o + BLK, :] = u
            row.append(u)
        for a in range(k + 1, n):
            for b in range(a, n):
                o = block_at(a, b) * BLK
                g[o:o + BLK, :] = g[o:o + BLK, :] - gram_like(row[a - k - 1], row[b - k - 1])


def own_part(g, row, col):
    a, b = row // 8, col // 2
    o = pl.multiple_of(block_at(a, b) * BLK + (row % 8) * 16, 16)
    v = g[pl.ds(o, 16), :]
    shifted = jnp.concatenate([v[:, 64:], v[:, :64]], axis=1)
    i = row * 16 + lax.broadcasted_iota(jnp.int32, (16, BLK), 0)
    j = col * 64 + lax.broadcasted_iota(jnp.int32, (16, BLK), 1)
    half = lax.broadcasted_iota(jnp.int32, (16, BLK), 1) * 0 + col % 2
    v = jnp.where(half == 1, shifted, v)
    return jnp.where(j >= i, v, 0.0)[:, :64]


def gram_body(cfg, tt_ref, ft_any, out_ref, ft_ref, tb, pf, sb, xb, gp, rc, hb, rx, zb, rz, gf, work, inv,
              ld_sem, sa_sem, ra_sem, sc_sem, rc_sem, sx_sem, rx_sem, sz_sem, rz_sem, sg_sem, rg_sem, ft_sem, col_sem):
    nx, ny, nz, jl, scale = cfg
    half = gp.shape[1]
    nq = nx * ny
    rows = half // nq
    g = lax.axis_index("grp")
    d = lax.axis_index("dev")
    x, c = g // 2, g % 2
    y, z = d // nz, d % nz
    q_own = x * ny + y

    def dev_id(gg, dd):
        return {"grp": gg, "dev": dd}

    ft_cp = pltpu.make_async_copy(ft_any, ft_ref, ft_sem)
    ft_cp.start()
    chunks = []
    for t in range(ny):
        cg = (y + t) % ny
        cp = pltpu.make_async_copy(tt_ref.at[:, pl.ds(pl.multiple_of(cg * BLK, BLK), BLK), :], tb.at[t], ld_sem.at[t])
        cp.start()
        chunks.append(cp)

    barrier = pltpu.get_barrier_semaphore()
    nbar = 0

    def sig(gg, dd):
        pl.semaphore_signal(barrier, inc=1, device_id=dev_id(gg, dd), device_id_type=MESH)

    for k in range(1, nz):
        sig(g, y * nz + (z + k) % nz)
        nbar += 1
    for kx in range(nx):
        for ky in range(ny):
            if (kx, ky) != (0, 0):
                sig(((x + kx) % nx) * 2 + c, ((y + ky) % ny) * nz + z)
                nbar += 1
    sig(x * 2 + 1 - c, d)
    nbar += 1

    zorder = sorted(range(nz), key=lambda k: (-min(k, nz - k), k))
    mine = pl.ds(pl.multiple_of(d * jl, jl), jl)
    jg = 256 // BLK
    sends = []
    ft_cp.wait()
    for t in range(ny):
        chunks[t].wait()

        def proj(i, carry):
            rhs = tb[t, pl.ds(i * jg, jg)].reshape(jg * BLK, tb.shape[-1])
            o = lax.dot_general(ft_ref[...], rhs, (((1,), (1,)), ((), ())), preferred_element_type=jnp.float32)
            for rg in range(nz):
                for jj in range(jg):
                    pf[pl.ds(pl.multiple_of(rg * jl * 8 + (i * jg + jj) * 8, 8), 8), :] = o[rg * 8:(rg + 1) * 8, jj * BLK:(jj + 1) * BLK]
            return carry

        lax.fori_loop(0, jl // jg, proj, 0)
        cg = (y + t) % ny
        for n, zo in enumerate(zorder):
            rg = (z + zo) % nz
            local = t == 0 and zo == 0
            for r in range(8):
                v = pf[pl.ds(pl.multiple_of(rg * jl * 8, 8) + r, jl, stride=8), :].astype(jnp.bfloat16)
                if local:
                    xb[mine, r * BLK:(r + 1) * BLK] = v
                else:
                    sb[t, n, :, r * BLK:(r + 1) * BLK] = v
            if t == 0 and n == 0:
                pl.semaphore_wait(barrier, nbar)
                for k in range(1, ny):
                    pl.semaphore_signal(col_sem.at[k], inc=1, device_id=dev_id(g, (y + k) % ny * nz + z), device_id_type=MESH)
            if t == 1 and n == 0:
                for k in range(1, ny):
                    pl.semaphore_wait(col_sem.at[k], 1)
            if not local:
                cp = pltpu.make_async_remote_copy(sb.at[t, n], xb.at[mine, :], sa_sem.at[t, n], ra_sem.at[d],
                                                  device_id=dev_id(g, cg * nz + rg), device_id_type=MESH)
                cp.start()
                sends.append(cp)

    partner = dev_id(x * 2 + 1 - c, d)

    def to_core(idx):
        at = pl.ds(pl.multiple_of(idx * (BLK // 2), BLK // 2), BLK // 2)
        return pltpu.make_async_remote_copy(gp.at[1 - c, at, :], rc.at[at, :], sc_sem.at[idx], rc_sem.at[idx],
                                            device_id=partner, device_id_type=MESH)

    for t in range(ny):
        ya = (y + ny - t) % ny
        for k in range(0 if t else 1, nz):
            src = ya * nz + (z + k) % nz
            landed = xb.at[pl.ds(pl.multiple_of(src * jl, jl), jl), :]
            pltpu.make_async_copy(landed, landed, ra_sem.at[src]).wait()

        def gram_block(u, carry, t=t):
            a = (y + ny - t) % ny
            b = (y + ny - u) % ny
            less = (b - a + ny - 1) // ny
            lo = b + (a - b) * less
            hi = a + b - lo
            idx = lo * 4 - lo * (lo - 1) // 2 + hi - lo
            xa = xb[pl.ds(pl.multiple_of(lo * BLK, BLK), BLK), :]
            xc = xb[pl.ds(pl.multiple_of(hi * BLK, BLK), BLK), :]
            o = lax.dot_general(xa, xc, (((1,), (1,)), ((), ())), preferred_element_type=jnp.float32) * scale
            at = pl.ds(pl.multiple_of(idx * (BLK // 2), BLK // 2), BLK // 2)
            gp[0, at, :] = o[:BLK // 2]
            gp[1, at, :] = o[BLK // 2:]
            to_core(idx).start()
            return carry

        lax.fori_loop(0, t + 1, gram_block, 0)
    own = pl.multiple_of(c * half, 8)
    other = pl.multiple_of((1 - c) * half, 8)
    for idx in range(10):
        to_core(idx).wait_recv()
    hb[...] = gp[c] + rc[...]

    plane = sorted(((kx, ky) for kx in range(nx) for ky in range(ny)), key=lambda k: min(k[0], nx - k[0]) + min(k[1], ny - k[1]))
    xy_cps = []
    for kx in range(nx):
        for ky in range(ny):
            if kx == 0 and ky == 0:
                continue
            px, py = (x + kx) % nx, (y + ky) % ny
            q = px * ny + py
            cp = pltpu.make_async_remote_copy(hb.at[pl.ds(pl.multiple_of(q * rows, 8), rows), :], rx.at[q_own],
                                              sx_sem.at[0, kx * ny + ky], rx_sem.at[0, q_own],
                                              device_id=dev_id(px * 2 + c, py * nz + z), device_id_type=MESH)
            cp.start()
            xy_cps.append(cp)
    rx[q_own] = hb[pl.ds(pl.multiple_of(q_own * rows, 8), rows), :]

    def wait_xy(k, carry):
        q = (q_own + k) % nq
        pltpu.make_async_copy(rx.at[q], rx.at[q], rx_sem.at[0, q]).wait()
        return carry

    lax.fori_loop(1, nq, wait_xy, 0)
    acc = rx[0]
    for q in range(1, nq):
        acc += rx[q]
    zb[...] = acc

    z_cps = []
    for kz in range(1, nz):
        pz = (z + kz) % nz
        cp = pltpu.make_async_remote_copy(zb, rz.at[z], sz_sem.at[kz], rz_sem.at[z],
                                          device_id=dev_id(g, y * nz + pz), device_id_type=MESH)
        cp.start()
        z_cps.append(cp)
    rz[z] = acc
    for kz in range(1, nz):
        pz = (z + kz) % nz
        pltpu.make_async_copy(rz.at[pz], rz.at[pz], rz_sem.at[pz]).wait()
    acc = rz[0]
    for k in range(1, nz):
        acc += rz[k]

    here = pl.ds(pl.multiple_of(own + q_own * rows, 8), rows)
    gf[here, :] = acc
    ag_cps = []
    for kx in range(nx):
        for ky in range(ny):
            if kx == 0 and ky == 0:
                continue
            px, py = (x + kx) % nx, (y + ky) % ny
            cp = pltpu.make_async_remote_copy(gf.at[here, :], gf.at[here, :],
                                              sx_sem.at[1, kx * ny + ky], rx_sem.at[1, q_own],
                                              device_id=dev_id(px * 2 + c, py * nz + z), device_id_type=MESH)
            cp.start()
            ag_cps.append(cp)

    forward = []
    for kx, ky in plane:
        q = ((x + kx) % nx) * ny + (y + ky) % ny
        piece = gf.at[pl.ds(pl.multiple_of(own + q * rows, 8), rows), :]
        if (kx, ky) != (0, 0):
            pltpu.make_async_copy(piece, piece, rx_sem.at[1, q]).wait()
        cp = pltpu.make_async_remote_copy(piece, piece, sg_sem.at[q], rg_sem.at[q],
                                          device_id=dev_id(x * 2 + 1 - c, d), device_id_type=MESH)
        cp.start()
        forward.append(cp)
    for q in range(nq):
        piece = gf.at[pl.ds(pl.multiple_of(other + q * rows, 8), rows), :]
        pltpu.make_async_copy(piece, piece, rg_sem.at[q]).wait()
    hb_rows = BLK // 2
    for idx in range(10):
        for h in range(2):
            work[idx * BLK + h * hb_rows:idx * BLK + (h + 1) * hb_rows, :] = gf[h * half + idx * hb_rows:h * half + (idx + 1) * hb_rows, :]
    cholesky_packed(work, inv)
    out_ref[...] = own_part(work, d, g)
    for idx in range(10):
        to_core(idx).wait_send()
    for cp in sends + xy_cps + z_cps + ag_cps + forward:
        cp.wait_send()


def triangle(tt, ft, nx, ny, nz, scale):
    jl, ks, ni = tt.shape
    n2 = jl * ny * nz
    nq = nx * ny
    half = 5 * BLK
    rows = half // nq
    cfg = (nx, ny, nz, jl, scale)
    f32, bf16 = jnp.float32, jnp.bfloat16
    dma = pltpu.SemaphoreType.DMA
    return pl.pallas_call(
        functools.partial(gram_body, cfg),
        out_shape=jax.ShapeDtypeStruct((n2 // (ny * nz), n2 // (2 * nx)), f32),
        in_specs=[pl.BlockSpec(memory_space=pltpu.MemorySpace.HBM)] * 2,
        out_specs=pl.BlockSpec(memory_space=pltpu.VMEM),
        scratch_shapes=[
            pltpu.VMEM(ft.shape, bf16),
            pltpu.VMEM((ny, jl, BLK, ni), bf16),
            pltpu.VMEM((nz * jl * 8, BLK), f32),
            pltpu.VMEM((ny, nz, jl, 8 * BLK), bf16),
            pltpu.VMEM((n2, 8 * BLK), bf16),
            pltpu.VMEM((2, half, BLK), f32),
            pltpu.VMEM((half, BLK), f32),
            pltpu.VMEM((half, BLK), f32),
            pltpu.VMEM((nq, rows, BLK), f32),
            pltpu.VMEM((rows, BLK), f32),
            pltpu.VMEM((nz, rows, BLK), f32),
            pltpu.VMEM((2 * half, BLK), f32),
            pltpu.VMEM((2 * half, BLK), f32),
            pltpu.VMEM((BLK, BLK), f32),
            dma((ny,)),
            dma((ny, nz)), dma((ny * nz,)),
            dma((10,)), dma((10,)),
            dma((2, nq)), dma((2, nq)),
            dma((nz,)), dma((nz,)),
            dma((nq,)), dma((nq,)),
            dma(()),
            pltpu.SemaphoreType.REGULAR((ny,)),
        ],
        compiler_params=pltpu.CompilerParams(collective_id=0, has_side_effects=True, vmem_limit_bytes=48 << 20),
    )(tt, ft)


def per_device(ny, tensor_slab, mode_factor):
    ni, jl, kl, s = tensor_slab.shape
    grp, dev = lax.axis_size("grp"), lax.axis_size("dev")
    tt = jnp.transpose(tensor_slab, (1, 2, 3, 0)).reshape(jl, kl * s, ni)
    row_total = mode_factor.shape[1] * kl * s * grp
    return triangle(tt, mode_factor.T, grp // 2, ny, dev // ny, 1.0 / row_total)


def solution(mesh, ny=NY):
    in_specs = (P(None, "dev", "grp", None), P())
    out_specs = P("dev", "grp")
    return jax.shard_map(
        functools.partial(per_device, ny), mesh=mesh, in_specs=in_specs, out_specs=out_specs, check_vma=False
    )
```

```python
import functools

import jax
import jax.numpy as jnp
from jax import lax
from jax.experimental import pallas as pl
from jax.experimental.pallas import tpu as pltpu
from jax.sharding import PartitionSpec as P

MESH = pl.DeviceIdType.MESH
BLK = 128
NY = 4
SUB = 16
STRIP = 32
PARTS = (16, 24)


def split3(v):
    hi = v.astype(jnp.bfloat16)
    rest = v - hi.astype(jnp.float32)
    mid = rest.astype(jnp.bfloat16)
    low = (rest - mid.astype(jnp.float32)).astype(jnp.bfloat16)
    return hi, mid, low


def gram_like(a, b):
    ah, am, al = split3(a)
    bh, bm, bl = split3(b)
    lhs = jnp.concatenate([ah, ah, am, ah, am, al], axis=0)
    rhs = jnp.concatenate([bh, bm, bh, bl, bm, bh], axis=0)
    return lax.dot_general(lhs, rhs, (((0,), (0,)), ((), ())), preferred_element_type=jnp.float32)


def spread(v, q):
    return jnp.broadcast_to(v[q:q + 1, :], (8, BLK))


def eliminate(rows, left, first):
    sub = lax.broadcasted_iota(jnp.int32, (8, BLK), 0)
    pieces = range(first, len(rows[0]))
    col = [{i: jnp.broadcast_to(rows[0][i][:, left + q:left + q + 1], (8, BLK)) for i in pieces if i > first or q < 8}
           for q in range(SUB)]
    piv = [jnp.ones((8, BLK), jnp.float32)] * 2

    def at(q, p):
        return spread(col[q][first + p // 8], p % 8)

    d = at(0, 0)
    for q in range(SUB):
        r = 1.0 / d
        piv[q // 8] = jnp.where(sub == q % 8, d, piv[q // 8])
        if q < SUB - 1:
            e = at(q, q + 1)
            d = at(q + 1, q + 1) - (e * e) * r
        mult = {i: v * r for i, v in col[q].items() if i >= first + q // 8}
        for p in range(q + 1, SUB):
            e = at(q, p)
            for i in col[p]:
                if i >= first + p // 8:
                    col[p][i] = col[p][i] - mult[i] * e
        here = first + q // 8
        for t in rows:
            e = spread(t[here], q % 8)
            for i in mult:
                if i > here:
                    t[i] = t[i] - mult[i] * e
                elif q % 8 < 7:
                    t[i] = t[i] - jnp.where(sub > q % 8, mult[i], 0.0) * e
    return [lax.rsqrt(v) for v in piv]


def factor_rows(rows, left):
    rows = [list(t) for t in rows]
    scales = []
    for first in range(0, len(rows[0]), 2):
        scales += eliminate(rows, left + first * 8, first)
    return [jnp.concatenate([v * s for v, s in zip(t, scales)], axis=0) for t in rows]


def block_at(a, b):
    return a * 4 - a * (a - 1) // 2 + b - a


def product(a, b):
    ah, am, al = split3(a)
    bh, bm, bl = split3(b)
    lhs = jnp.concatenate([ah, ah, am, ah, am, al], axis=1)
    rhs = jnp.concatenate([bh, bm, bh, bl, bm, bh], axis=0)
    return lax.dot_general(lhs, rhs, (((1,), (0,)), ((), ())), preferred_element_type=jnp.float32)


def cholesky_packed(g, inv):
    n = 4
    eye = (lax.broadcasted_iota(jnp.int32, (BLK, BLK), 0) == lax.broadcasted_iota(jnp.int32, (BLK, BLK), 1)).astype(jnp.float32)
    def panel(k, b):
        o = block_at(k, b) * BLK
        g[o:o + BLK, :] = product(inv[k % 2], g[o:o + BLK, :])

    def update(k, a, b):
        o, oa, ob = (block_at(*ab) * BLK for ab in ((a, b), (k, a), (k, b)))
        g[o:o + BLK, :] = g[o:o + BLK, :] - gram_like(g[oa:oa + BLK, :], g[ob:ob + BLK, :])

    for k in range(n):
        base = block_at(k, k) * BLK
        last = k == n - 1
        way = inv.at[k % 2]
        if not last:
            way[...] = eye
        refs = [(g, base)] if last else [(g, base), (way, 0)]
        for s in range(BLK // STRIP):
            at = s * STRIP
            tiles = [[r[o + at + i:o + at + i + 8, :] for i in range(0, STRIP, 8)] for r, o in refs]
            done = factor_rows(tiles, at)
            for (r, o), v in zip(refs, done):
                r[o + at:o + at + STRIP, :] = v
            end = at + STRIP
            if end < BLK:
                both = done[0] if last else jnp.concatenate(done, axis=1)
                upd = gram_like(done[0], both)
                for i, (r, o) in enumerate(refs):
                    r[o + end:o + BLK, :] = r[o + end:o + BLK, :] - upd[end:, i * BLK:(i + 1) * BLK]
        if last:
            break
        for b in range(k + 1, n):
            panel(k, b)
        for a in range(k + 1, n):
            for b in range(a, n):
                update(k, a, b)


def own_part(g, row, col):
    a, b = row // 8, col // 2
    o = pl.multiple_of(block_at(a, b) * BLK + (row % 8) * 16, 16)
    v = g[pl.ds(o, 16), :]
    shifted = jnp.concatenate([v[:, 64:], v[:, :64]], axis=1)
    i = row * 16 + lax.broadcasted_iota(jnp.int32, (16, BLK), 0)
    j = col * 64 + lax.broadcasted_iota(jnp.int32, (16, BLK), 1)
    half = lax.broadcasted_iota(jnp.int32, (16, BLK), 1) * 0 + col % 2
    v = jnp.where(half == 1, shifted, v)
    return jnp.where(j >= i, v, 0.0)[:, :64]


def gram_body(cfg, tt_ref, ft_any, out_ref, ft_ref, tb, pf, sb, xb, gp, rc, hb, rx, zb, rz, gf, work, inv,
              ld_sem, sa_sem, ra_sem, sc_sem, rc_sem, sx_sem, rx_sem, sz_sem, rz_sem, sg_sem, rg_sem, ft_sem, col_sem):
    nx, ny, nz, jl, scale = cfg
    half = gp.shape[1]
    nq = nx * ny
    rows = half // nq
    g = lax.axis_index("grp")
    d = lax.axis_index("dev")
    x, c = g // 2, g % 2
    y, z = d // nz, d % nz
    q_own = x * ny + y

    def dev_id(gg, dd):
        return {"grp": gg, "dev": dd}

    ft_cp = pltpu.make_async_copy(ft_any, ft_ref, ft_sem)
    ft_cp.start()
    chunks = []
    for t in range(ny):
        cg = (y + t) % ny
        cp = pltpu.make_async_copy(tt_ref.at[:, pl.ds(pl.multiple_of(cg * BLK, BLK), BLK), :], tb.at[t], ld_sem.at[t])
        cp.start()
        chunks.append(cp)

    barrier = pltpu.get_barrier_semaphore()
    nbar = 0

    def sig(gg, dd):
        pl.semaphore_signal(barrier, inc=1, device_id=dev_id(gg, dd), device_id_type=MESH)

    for k in range(1, nz):
        sig(g, y * nz + (z + k) % nz)
        nbar += 1
    for kx in range(nx):
        for ky in range(ny):
            if (kx, ky) != (0, 0):
                sig(((x + kx) % nx) * 2 + c, ((y + ky) % ny) * nz + z)
                nbar += 1
    sig(x * 2 + 1 - c, d)
    nbar += 1

    zorder = sorted(range(nz), key=lambda k: (-min(k, nz - k), k))
    mine = pl.ds(pl.multiple_of(d * jl, jl), jl)
    jg = 256 // BLK
    sends = []
    ft_cp.wait()
    for t in range(ny):
        chunks[t].wait()

        def proj(i, carry):
            rhs = tb[t, pl.ds(i * jg, jg)].reshape(jg * BLK, tb.shape[-1])
            o = lax.dot_general(ft_ref[...], rhs, (((1,), (1,)), ((), ())), preferred_element_type=jnp.float32)
            for rg in range(nz):
                for jj in range(jg):
                    pf[pl.ds(pl.multiple_of(rg * jl * 8 + (i * jg + jj) * 8, 8), 8), :] = o[rg * 8:(rg + 1) * 8, jj * BLK:(jj + 1) * BLK]
            return carry

        lax.fori_loop(0, jl // jg, proj, 0)
        cg = (y + t) % ny
        for n, zo in enumerate(zorder):
            rg = (z + zo) % nz
            local = t == 0 and zo == 0
            for r in range(8):
                v = pf[pl.ds(pl.multiple_of(rg * jl * 8, 8) + r, jl, stride=8), :].astype(jnp.bfloat16)
                if local:
                    xb[mine, r * BLK:(r + 1) * BLK] = v
                else:
                    sb[t, n, :, r * BLK:(r + 1) * BLK] = v
            if t == 0 and n == 0:
                pl.semaphore_wait(barrier, nbar)
                for k in range(1, ny):
                    pl.semaphore_signal(col_sem.at[k], inc=1, device_id=dev_id(g, (y + k) % ny * nz + z), device_id_type=MESH)
            if t == 1 and n == 0:
                for k in range(1, ny):
                    pl.semaphore_wait(col_sem.at[k], 1)
            if not local:
                cp = pltpu.make_async_remote_copy(sb.at[t, n], xb.at[mine, :], sa_sem.at[t, n], ra_sem.at[d],
                                                  device_id=dev_id(g, cg * nz + rg), device_id_type=MESH)
                cp.start()
                sends.append(cp)

    partner = dev_id(x * 2 + 1 - c, d)

    def to_core(idx):
        at = pl.ds(pl.multiple_of(idx * (BLK // 2), BLK // 2), BLK // 2)
        return pltpu.make_async_remote_copy(gp.at[1 - c, at, :], rc.at[at, :], sc_sem.at[idx], rc_sem.at[idx],
                                            device_id=partner, device_id_type=MESH)

    for t in range(ny):
        ya = (y + ny - t) % ny
        for k in range(0 if t else 1, nz):
            src = ya * nz + (z + k) % nz
            landed = xb.at[pl.ds(pl.multiple_of(src * jl, jl), jl), :]
            pltpu.make_async_copy(landed, landed, ra_sem.at[src]).wait()

        def gram_block(u, carry, t=t):
            a = (y + ny - t) % ny
            b = (y + ny - u) % ny
            less = (b - a + ny - 1) // ny
            lo = b + (a - b) * less
            hi = a + b - lo
            idx = lo * 4 - lo * (lo - 1) // 2 + hi - lo
            xa = xb[pl.ds(pl.multiple_of(lo * BLK, BLK), BLK), :]
            xc = xb[pl.ds(pl.multiple_of(hi * BLK, BLK), BLK), :]
            o = lax.dot_general(xa, xc, (((1,), (1,)), ((), ())), preferred_element_type=jnp.float32) * scale
            at = pl.ds(pl.multiple_of(idx * (BLK // 2), BLK // 2), BLK // 2)
            gp[0, at, :] = o[:BLK // 2]
            gp[1, at, :] = o[BLK // 2:]
            to_core(idx).start()
            return carry

        lax.fori_loop(0, t + 1, gram_block, 0)
    own = pl.multiple_of(c * half, 8)
    other = pl.multiple_of((1 - c) * half, 8)
    for idx in range(10):
        to_core(idx).wait_recv()
    hb[...] = gp[c] + rc[...]

    plane = sorted(((kx, ky) for kx in range(nx) for ky in range(ny)), key=lambda k: min(k[0], nx - k[0]) + min(k[1], ny - k[1]))
    parts = []
    at_row = 0
    for n in PARTS:
        parts.append((at_row, n))
        at_row += n
    later = []

    def send(src, dst, s_sem, r_sem, to):
        cp = pltpu.make_async_remote_copy(src, dst, s_sem, r_sem, device_id=to, device_id_type=MESH)
        cp.start()
        later.append(cp)

    def at_peer(kx, ky):
        px, py = (x + kx) % nx, (y + ky) % ny
        return px * ny + py, dev_id(px * 2 + c, py * nz + z)

    def held(base, r0, n):
        return gf.at[pl.ds(pl.multiple_of(base + r0, 8), n), :]

    for p, (r0, n) in enumerate(parts):
        for kx, ky in plane[1:]:
            q, to = at_peer(kx, ky)
            send(hb.at[pl.ds(pl.multiple_of(q * rows + r0, 8), n), :], rx.at[q_own, pl.ds(r0, n)],
                 sx_sem.at[0, p, kx * ny + ky], rx_sem.at[0, p, q_own], to)
    rx[q_own] = hb[pl.ds(pl.multiple_of(q_own * rows, 8), rows), :]
    for p, (r0, n) in enumerate(parts):
        def wait_xy(k, carry, p=p, r0=r0, n=n):
            q = (q_own + k) % nq
            piece = rx.at[q, pl.ds(r0, n)]
            pltpu.make_async_copy(piece, piece, rx_sem.at[0, p, q]).wait()
            return carry

        lax.fori_loop(1, nq, wait_xy, 0)
        acc = rx[0, r0:r0 + n]
        for q in range(1, nq):
            acc += rx[q, r0:r0 + n]
        zb[r0:r0 + n] = acc
        for kz in range(1, nz):
            send(zb.at[pl.ds(r0, n)], rz.at[z, pl.ds(r0, n)], sz_sem.at[p, kz], rz_sem.at[p, z],
                 dev_id(g, y * nz + (z + kz) % nz))
        rz[z, r0:r0 + n] = acc
    for p, (r0, n) in enumerate(parts):
        for kz in range(1, nz):
            piece = rz.at[(z + kz) % nz, pl.ds(r0, n)]
            pltpu.make_async_copy(piece, piece, rz_sem.at[p, (z + kz) % nz]).wait()
        acc = rz[0, r0:r0 + n]
        for k in range(1, nz):
            acc += rz[k, r0:r0 + n]
        gf[pl.ds(pl.multiple_of(own + q_own * rows + r0, 8), n), :] = acc
        here = held(own + q_own * rows, r0, n)
        for kx, ky in plane[1:]:
            send(here, here, sx_sem.at[1, p, kx * ny + ky], rx_sem.at[1, p, q_own], at_peer(kx, ky)[1])
    for p, (r0, n) in enumerate(parts):
        for kx, ky in plane:
            q = at_peer(kx, ky)[0]
            piece = held(own + q * rows, r0, n)
            if (kx, ky) != (0, 0):
                pltpu.make_async_copy(piece, piece, rx_sem.at[1, p, q]).wait()
            send(piece, piece, sg_sem.at[p, q], rg_sem.at[p, q], partner)
    for p, (r0, n) in enumerate(parts):
        for q in range(nq):
            piece = held(other + q * rows, r0, n)
            pltpu.make_async_copy(piece, piece, rg_sem.at[p, q]).wait()
    hb_rows = BLK // 2
    for idx in range(10):
        for h in range(2):
            work[idx * BLK + h * hb_rows:idx * BLK + (h + 1) * hb_rows, :] = gf[h * half + idx * hb_rows:h * half + (idx + 1) * hb_rows, :]
    cholesky_packed(work, inv)
    out_ref[...] = own_part(work, d, g)
    for idx in range(10):
        to_core(idx).wait_send()
    for cp in sends + later:
        cp.wait_send()


def triangle(tt, ft, nx, ny, nz, scale):
    jl, ks, ni = tt.shape
    n2 = jl * ny * nz
    nq = nx * ny
    half = 5 * BLK
    rows = half // nq
    np_ = len(PARTS)
    cfg = (nx, ny, nz, jl, scale)
    f32, bf16 = jnp.float32, jnp.bfloat16
    dma = pltpu.SemaphoreType.DMA
    return pl.pallas_call(
        functools.partial(gram_body, cfg),
        out_shape=jax.ShapeDtypeStruct((n2 // (ny * nz), n2 // (2 * nx)), f32),
        in_specs=[pl.BlockSpec(memory_space=pltpu.MemorySpace.HBM)] * 2,
        out_specs=pl.BlockSpec(memory_space=pltpu.VMEM),
        scratch_shapes=[
            pltpu.VMEM(ft.shape, bf16),
            pltpu.VMEM((ny, jl, BLK, ni), bf16),
            pltpu.VMEM((nz * jl * 8, BLK), f32),
            pltpu.VMEM((ny, nz, jl, 8 * BLK), bf16),
            pltpu.VMEM((n2, 8 * BLK), bf16),
            pltpu.VMEM((2, half, BLK), f32),
            pltpu.VMEM((half, BLK), f32),
            pltpu.VMEM((half, BLK), f32),
            pltpu.VMEM((nq, rows, BLK), f32),
            pltpu.VMEM((rows, BLK), f32),
            pltpu.VMEM((nz, rows, BLK), f32),
            pltpu.VMEM((2 * half, BLK), f32),
            pltpu.VMEM((2 * half, BLK), f32),
            pltpu.VMEM((2, BLK, BLK), f32),
            dma((ny,)),
            dma((ny, nz)), dma((ny * nz,)),
            dma((10,)), dma((10,)),
            dma((2, np_, nq)), dma((2, np_, nq)),
            dma((np_, nz)), dma((np_, nz)),
            dma((np_, nq)), dma((np_, nq)),
            dma(()),
            pltpu.SemaphoreType.REGULAR((ny,)),
        ],
        compiler_params=pltpu.CompilerParams(collective_id=0, has_side_effects=True, vmem_limit_bytes=48 << 20),
    )(tt, ft)


def per_device(ny, tensor_slab, mode_factor):
    ni, jl, kl, s = tensor_slab.shape
    grp, dev = lax.axis_size("grp"), lax.axis_size("dev")
    tt = jnp.transpose(tensor_slab, (1, 2, 3, 0)).reshape(jl, kl * s, ni)
    row_total = mode_factor.shape[1] * kl * s * grp
    return triangle(tt, mode_factor.T, grp // 2, ny, dev // ny, 1.0 / row_total)


def solution(mesh, ny=NY):
    in_specs = (P(None, "dev", "grp", None), P())
    out_specs = P("dev", "grp")
    return jax.shard_map(
        functools.partial(per_device, ny), mesh=mesh, in_specs=in_specs, out_specs=out_specs, check_vma=False
    )
```

```python
import functools

import jax
import jax.numpy as jnp
from jax import lax
from jax.experimental import pallas as pl
from jax.experimental.pallas import tpu as pltpu
from jax.sharding import PartitionSpec as P

MESH = pl.DeviceIdType.MESH
BLK = 128
NY = 4
SUB = 16
STRIP = 32
PARTS = (16, 24)


def split3(v):
    hi = v.astype(jnp.bfloat16)
    rest = v - hi.astype(jnp.float32)
    mid = rest.astype(jnp.bfloat16)
    low = (rest - mid.astype(jnp.float32)).astype(jnp.bfloat16)
    return hi, mid, low


def gram_like(a, b):
    ah, am, al = split3(a)
    bh, bm, bl = split3(b)
    lhs = jnp.concatenate([ah, ah, am, ah, am, al], axis=0)
    rhs = jnp.concatenate([bh, bm, bh, bl, bm, bh], axis=0)
    return lax.dot_general(lhs, rhs, (((0,), (0,)), ((), ())), preferred_element_type=jnp.float32)


def spread(v, q):
    return jnp.broadcast_to(v[q:q + 1, :], (8, BLK))


def eliminate(rows, left, first):
    sub = lax.broadcasted_iota(jnp.int32, (8, BLK), 0)
    pieces = range(first, len(rows[0]))
    col = [{i: jnp.broadcast_to(rows[0][i][:, left + q:left + q + 1], (8, BLK)) for i in pieces if i > first or q < 8}
           for q in range(SUB)]
    piv = [jnp.ones((8, BLK), jnp.float32)] * 2

    def at(q, p):
        return spread(col[q][first + p // 8], p % 8)

    d = at(0, 0)
    for q in range(SUB):
        r = 1.0 / d
        piv[q // 8] = jnp.where(sub == q % 8, d, piv[q // 8])
        if q < SUB - 1:
            e = at(q, q + 1)
            d = at(q + 1, q + 1) - (e * e) * r
        mult = {i: v * r for i, v in col[q].items() if i >= first + q // 8}
        for p in range(q + 1, SUB):
            e = at(q, p)
            for i in col[p]:
                if i >= first + p // 8:
                    col[p][i] = col[p][i] - mult[i] * e
        here = first + q // 8
        for t in rows:
            e = spread(t[here], q % 8)
            for i in mult:
                if i > here:
                    t[i] = t[i] - mult[i] * e
                elif q % 8 < 7:
                    t[i] = t[i] - jnp.where(sub > q % 8, mult[i], 0.0) * e
    return [lax.rsqrt(v) for v in piv]


def factor_rows(rows, left):
    rows = [list(t) for t in rows]
    scales = []
    for first in range(0, len(rows[0]), 2):
        scales += eliminate(rows, left + first * 8, first)
    return [jnp.concatenate([v * s for v, s in zip(t, scales)], axis=0) for t in rows]


def block_at(a, b):
    return a * 4 - a * (a - 1) // 2 + b - a


def product(a, b):
    ah, am, al = split3(a)
    bh, bm, bl = split3(b)
    lhs = jnp.concatenate([ah, ah, am, ah, am, al], axis=1)
    rhs = jnp.concatenate([bh, bm, bh, bl, bm, bh], axis=0)
    return lax.dot_general(lhs, rhs, (((1,), (0,)), ((), ())), preferred_element_type=jnp.float32)


def cholesky_packed(g, inv, row, col):
    n = 4
    mine, own_strip = row // 8, row % 8 // (STRIP // 16)
    eye = (lax.broadcasted_iota(jnp.int32, (BLK, BLK), 0) == lax.broadcasted_iota(jnp.int32, (BLK, BLK), 1)).astype(jnp.float32)
    def panel(k, b):
        o = block_at(k, b) * BLK
        g[o:o + BLK, :] = product(inv[k % 2], g[o:o + BLK, :])

    def update(k, a, b):
        o, oa, ob = (block_at(*ab) * BLK for ab in ((a, b), (k, a), (k, b)))
        g[o:o + BLK, :] = g[o:o + BLK, :] - gram_like(g[oa:oa + BLK, :], g[ob:ob + BLK, :])

    def strip(k, refs, s):
        at = s * STRIP
        tiles = [[r[o + at + i:o + at + i + 8, :] for i in range(0, STRIP, 8)] for r, o in refs]
        done = factor_rows(tiles, at)
        for (r, o), v in zip(refs, done):
            r[o + at:o + at + STRIP, :] = v
        end = at + STRIP
        if end < BLK:
            both = jnp.concatenate(done, axis=1) if len(done) > 1 else done[0]
            upd = gram_like(done[0], both)
            for i, (r, o) in enumerate(refs):
                r[o + end:o + BLK, :] = r[o + end:o + BLK, :] - upd[end:, i * BLK:(i + 1) * BLK]

    def block_row(k):
        refs = [(g, block_at(k, k) * BLK)]
        if k < n - 1:
            inv[k % 2] = eye
            refs.append((inv.at[k % 2], 0))
        for s in range(BLK // STRIP):
            pl.when((mine - k) * (BLK // STRIP) + own_strip >= s)(functools.partial(strip, k, refs, s))
        for b in range(k + 1, n):
            panel(k, b)

        if k < n - 1:
            @pl.when(mine > k)
            def _():
                for a in range(k + 1, n):
                    for b in range(a, n):
                        update(k, a, b)

    @pl.when(col // 2 >= mine)
    def _():
        for k in range(n):
            pl.when(mine >= k)(functools.partial(block_row, k))


def own_part(g, row, col):
    a, b = row // 8, col // 2
    o = pl.multiple_of(block_at(a, b) * BLK + (row % 8) * 16, 16)
    v = g[pl.ds(o, 16), :]
    shifted = jnp.concatenate([v[:, 64:], v[:, :64]], axis=1)
    i = row * 16 + lax.broadcasted_iota(jnp.int32, (16, BLK), 0)
    j = col * 64 + lax.broadcasted_iota(jnp.int32, (16, BLK), 1)
    half = lax.broadcasted_iota(jnp.int32, (16, BLK), 1) * 0 + col % 2
    v = jnp.where(half == 1, shifted, v)
    return jnp.where(j >= i, v, 0.0)[:, :64]


def gram_body(cfg, tt_ref, ft_any, out_ref, ft_ref, tb, pf, sb, xb, gp, rc, hb, rx, zb, rz, gf, work, inv,
              ld_sem, sa_sem, ra_sem, sc_sem, rc_sem, sx_sem, rx_sem, sz_sem, rz_sem, sg_sem, rg_sem, ft_sem, col_sem):
    nx, ny, nz, jl, scale = cfg
    half = gp.shape[1]
    nq = nx * ny
    rows = half // nq
    g = lax.axis_index("grp")
    d = lax.axis_index("dev")
    x, c = g // 2, g % 2
    y, z = d // nz, d % nz
    q_own = x * ny + y

    def dev_id(gg, dd):
        return {"grp": gg, "dev": dd}

    ft_cp = pltpu.make_async_copy(ft_any, ft_ref, ft_sem)
    ft_cp.start()
    chunks = []
    for t in range(ny):
        cg = (y + t) % ny
        cp = pltpu.make_async_copy(tt_ref.at[:, pl.ds(pl.multiple_of(cg * BLK, BLK), BLK), :], tb.at[t], ld_sem.at[t])
        cp.start()
        chunks.append(cp)

    barrier = pltpu.get_barrier_semaphore()
    nbar = 0

    def sig(gg, dd):
        pl.semaphore_signal(barrier, inc=1, device_id=dev_id(gg, dd), device_id_type=MESH)

    for k in range(1, nz):
        sig(g, y * nz + (z + k) % nz)
        nbar += 1
    for kx in range(nx):
        for ky in range(ny):
            if (kx, ky) != (0, 0):
                sig(((x + kx) % nx) * 2 + c, ((y + ky) % ny) * nz + z)
                nbar += 1
    sig(x * 2 + 1 - c, d)
    nbar += 1

    zorder = sorted(range(nz), key=lambda k: (-min(k, nz - k), k))
    mine = pl.ds(pl.multiple_of(d * jl, jl), jl)
    jg = 256 // BLK
    sends = []
    ft_cp.wait()
    for t in range(ny):
        chunks[t].wait()

        def proj(i, carry):
            rhs = tb[t, pl.ds(i * jg, jg)].reshape(jg * BLK, tb.shape[-1])
            o = lax.dot_general(ft_ref[...], rhs, (((1,), (1,)), ((), ())), preferred_element_type=jnp.float32)
            for rg in range(nz):
                for jj in range(jg):
                    pf[pl.ds(pl.multiple_of(rg * jl * 8 + (i * jg + jj) * 8, 8), 8), :] = o[rg * 8:(rg + 1) * 8, jj * BLK:(jj + 1) * BLK]
            return carry

        lax.fori_loop(0, jl // jg, proj, 0)
        cg = (y + t) % ny
        for n, zo in enumerate(zorder):
            rg = (z + zo) % nz
            local = t == 0 and zo == 0
            for r in range(8):
                v = pf[pl.ds(pl.multiple_of(rg * jl * 8, 8) + r, jl, stride=8), :].astype(jnp.bfloat16)
                if local:
                    xb[mine, r * BLK:(r + 1) * BLK] = v
                else:
                    sb[t, n, :, r * BLK:(r + 1) * BLK] = v
            if t == 0 and n == 0:
                pl.semaphore_wait(barrier, nbar)
                for k in range(1, ny):
                    pl.semaphore_signal(col_sem.at[k], inc=1, device_id=dev_id(g, (y + k) % ny * nz + z), device_id_type=MESH)
            if t == 1 and n == 0:
                for k in range(1, ny):
                    pl.semaphore_wait(col_sem.at[k], 1)
            if not local:
                cp = pltpu.make_async_remote_copy(sb.at[t, n], xb.at[mine, :], sa_sem.at[t, n], ra_sem.at[d],
                                                  device_id=dev_id(g, cg * nz + rg), device_id_type=MESH)
                cp.start()
                sends.append(cp)

    partner = dev_id(x * 2 + 1 - c, d)

    def to_core(idx):
        at = pl.ds(pl.multiple_of(idx * (BLK // 2), BLK // 2), BLK // 2)
        return pltpu.make_async_remote_copy(gp.at[1 - c, at, :], rc.at[at, :], sc_sem.at[idx], rc_sem.at[idx],
                                            device_id=partner, device_id_type=MESH)

    for t in range(ny):
        ya = (y + ny - t) % ny
        for k in range(0 if t else 1, nz):
            src = ya * nz + (z + k) % nz
            landed = xb.at[pl.ds(pl.multiple_of(src * jl, jl), jl), :]
            pltpu.make_async_copy(landed, landed, ra_sem.at[src]).wait()

        def gram_block(u, carry, t=t):
            a = (y + ny - t) % ny
            b = (y + ny - u) % ny
            less = (b - a + ny - 1) // ny
            lo = b + (a - b) * less
            hi = a + b - lo
            idx = lo * 4 - lo * (lo - 1) // 2 + hi - lo
            xa = xb[pl.ds(pl.multiple_of(lo * BLK, BLK), BLK), :]
            xc = xb[pl.ds(pl.multiple_of(hi * BLK, BLK), BLK), :]
            o = lax.dot_general(xa, xc, (((1,), (1,)), ((), ())), preferred_element_type=jnp.float32) * scale
            at = pl.ds(pl.multiple_of(idx * (BLK // 2), BLK // 2), BLK // 2)
            gp[0, at, :] = o[:BLK // 2]
            gp[1, at, :] = o[BLK // 2:]
            to_core(idx).start()
            return carry

        lax.fori_loop(0, t + 1, gram_block, 0)
    own = pl.multiple_of(c * half, 8)
    other = pl.multiple_of((1 - c) * half, 8)
    for idx in range(10):
        to_core(idx).wait_recv()
    hb[...] = gp[c] + rc[...]

    plane = sorted(((kx, ky) for kx in range(nx) for ky in range(ny)), key=lambda k: min(k[0], nx - k[0]) + min(k[1], ny - k[1]))
    parts = []
    at_row = 0
    for n in PARTS:
        parts.append((at_row, n))
        at_row += n
    later = []

    def send(src, dst, s_sem, r_sem, to):
        cp = pltpu.make_async_remote_copy(src, dst, s_sem, r_sem, device_id=to, device_id_type=MESH)
        cp.start()
        later.append(cp)

    def at_peer(kx, ky):
        px, py = (x + kx) % nx, (y + ky) % ny
        return px * ny + py, dev_id(px * 2 + c, py * nz + z)

    def held(base, r0, n):
        return gf.at[pl.ds(pl.multiple_of(base + r0, 8), n), :]

    for p, (r0, n) in enumerate(parts):
        for kx, ky in plane[1:]:
            q, to = at_peer(kx, ky)
            send(hb.at[pl.ds(pl.multiple_of(q * rows + r0, 8), n), :], rx.at[q_own, pl.ds(r0, n)],
                 sx_sem.at[0, p, kx * ny + ky], rx_sem.at[0, p, q_own], to)
    rx[q_own] = hb[pl.ds(pl.multiple_of(q_own * rows, 8), rows), :]
    for p, (r0, n) in enumerate(parts):
        def wait_xy(k, carry, p=p, r0=r0, n=n):
            q = (q_own + k) % nq
            piece = rx.at[q, pl.ds(r0, n)]
            pltpu.make_async_copy(piece, piece, rx_sem.at[0, p, q]).wait()
            return carry

        lax.fori_loop(1, nq, wait_xy, 0)
        acc = rx[0, r0:r0 + n]
        for q in range(1, nq):
            acc += rx[q, r0:r0 + n]
        zb[r0:r0 + n] = acc
        for kz in range(1, nz):
            send(zb.at[pl.ds(r0, n)], rz.at[z, pl.ds(r0, n)], sz_sem.at[p, kz], rz_sem.at[p, z],
                 dev_id(g, y * nz + (z + kz) % nz))
        rz[z, r0:r0 + n] = acc
    for p, (r0, n) in enumerate(parts):
        for kz in range(1, nz):
            piece = rz.at[(z + kz) % nz, pl.ds(r0, n)]
            pltpu.make_async_copy(piece, piece, rz_sem.at[p, (z + kz) % nz]).wait()
        acc = rz[0, r0:r0 + n]
        for k in range(1, nz):
            acc += rz[k, r0:r0 + n]
        gf[pl.ds(pl.multiple_of(own + q_own * rows + r0, 8), n), :] = acc
        here = held(own + q_own * rows, r0, n)
        for kx, ky in plane[1:]:
            send(here, here, sx_sem.at[1, p, kx * ny + ky], rx_sem.at[1, p, q_own], at_peer(kx, ky)[1])
    for p, (r0, n) in enumerate(parts):
        for kx, ky in plane:
            q = at_peer(kx, ky)[0]
            piece = held(own + q * rows, r0, n)
            if (kx, ky) != (0, 0):
                pltpu.make_async_copy(piece, piece, rx_sem.at[1, p, q]).wait()
            send(piece, piece, sg_sem.at[p, q], rg_sem.at[p, q], partner)
    for p, (r0, n) in enumerate(parts):
        for q in range(nq):
            piece = held(other + q * rows, r0, n)
            pltpu.make_async_copy(piece, piece, rg_sem.at[p, q]).wait()
    hb_rows = BLK // 2
    for idx in range(10):
        for h in range(2):
            work[idx * BLK + h * hb_rows:idx * BLK + (h + 1) * hb_rows, :] = gf[h * half + idx * hb_rows:h * half + (idx + 1) * hb_rows, :]
    cholesky_packed(work, inv, d, g)
    out_ref[...] = own_part(work, d, g)
    for idx in range(10):
        to_core(idx).wait_send()
    for cp in sends + later:
        cp.wait_send()


def triangle(tt, ft, nx, ny, nz, scale):
    jl, ks, ni = tt.shape
    n2 = jl * ny * nz
    nq = nx * ny
    half = 5 * BLK
    rows = half // nq
    np_ = len(PARTS)
    cfg = (nx, ny, nz, jl, scale)
    f32, bf16 = jnp.float32, jnp.bfloat16
    dma = pltpu.SemaphoreType.DMA
    return pl.pallas_call(
        functools.partial(gram_body, cfg),
        out_shape=jax.ShapeDtypeStruct((n2 // (ny * nz), n2 // (2 * nx)), f32),
        in_specs=[pl.BlockSpec(memory_space=pltpu.MemorySpace.HBM)] * 2,
        out_specs=pl.BlockSpec(memory_space=pltpu.VMEM),
        scratch_shapes=[
            pltpu.VMEM(ft.shape, bf16),
            pltpu.VMEM((ny, jl, BLK, ni), bf16),
            pltpu.VMEM((nz * jl * 8, BLK), f32),
            pltpu.VMEM((ny, nz, jl, 8 * BLK), bf16),
            pltpu.VMEM((n2, 8 * BLK), bf16),
            pltpu.VMEM((2, half, BLK), f32),
            pltpu.VMEM((half, BLK), f32),
            pltpu.VMEM((half, BLK), f32),
            pltpu.VMEM((nq, rows, BLK), f32),
            pltpu.VMEM((rows, BLK), f32),
            pltpu.VMEM((nz, rows, BLK), f32),
            pltpu.VMEM((2 * half, BLK), f32),
            pltpu.VMEM((2 * half, BLK), f32),
            pltpu.VMEM((2, BLK, BLK), f32),
            dma((ny,)),
            dma((ny, nz)), dma((ny * nz,)),
            dma((10,)), dma((10,)),
            dma((2, np_, nq)), dma((2, np_, nq)),
            dma((np_, nz)), dma((np_, nz)),
            dma((np_, nq)), dma((np_, nq)),
            dma(()),
            pltpu.SemaphoreType.REGULAR((ny,)),
        ],
        compiler_params=pltpu.CompilerParams(collective_id=0, has_side_effects=True, vmem_limit_bytes=48 << 20),
    )(tt, ft)


def per_device(ny, tensor_slab, mode_factor):
    ni, jl, kl, s = tensor_slab.shape
    grp, dev = lax.axis_size("grp"), lax.axis_size("dev")
    tt = jnp.transpose(tensor_slab, (1, 2, 3, 0)).reshape(jl, kl * s, ni)
    row_total = mode_factor.shape[1] * kl * s * grp
    return triangle(tt, mode_factor.T, grp // 2, ny, dev // ny, 1.0 / row_total)


def solution(mesh, ny=NY):
    in_specs = (P(None, "dev", "grp", None), P())
    out_specs = P("dev", "grp")
    return jax.shard_map(
        functools.partial(per_device, ny), mesh=mesh, in_specs=in_specs, out_specs=out_specs, check_vma=False
    )
```

```python
import functools

import jax
import jax.numpy as jnp
from jax import lax
from jax.experimental import pallas as pl
from jax.experimental.pallas import tpu as pltpu
from jax.sharding import PartitionSpec as P

MESH = pl.DeviceIdType.MESH
BLK = 128
NY = 4
SUB = 16
STRIP = 32
PARTS = (16, 24)


def split3(v):
    hi = v.astype(jnp.bfloat16)
    rest = v - hi.astype(jnp.float32)
    mid = rest.astype(jnp.bfloat16)
    low = (rest - mid.astype(jnp.float32)).astype(jnp.bfloat16)
    return hi, mid, low


def gram_like(a, b):
    ah, am, al = split3(a)
    bh, bm, bl = split3(b)
    lhs = jnp.concatenate([ah, ah, am, ah, am, al], axis=0)
    rhs = jnp.concatenate([bh, bm, bh, bl, bm, bh], axis=0)
    return lax.dot_general(lhs, rhs, (((0,), (0,)), ((), ())), preferred_element_type=jnp.float32)


def spread(v, q):
    return jnp.broadcast_to(v[q:q + 1, :], (8, BLK))


def eliminate(rows, left, first):
    sub = lax.broadcasted_iota(jnp.int32, (8, BLK), 0)
    pieces = range(first, len(rows[0]))
    col = [{i: jnp.broadcast_to(rows[0][i][:, left + q:left + q + 1], (8, BLK)) for i in pieces if i > first or q < 8}
           for q in range(SUB)]
    piv = [jnp.ones((8, BLK), jnp.float32)] * 2

    def at(q, p):
        return spread(col[q][first + p // 8], p % 8)

    d = at(0, 0)
    for q in range(SUB):
        r = 1.0 / d
        piv[q // 8] = jnp.where(sub == q % 8, d, piv[q // 8])
        if q < SUB - 1:
            e = at(q, q + 1)
            d = at(q + 1, q + 1) - (e * e) * r
        mult = {i: v * r for i, v in col[q].items() if i >= first + q // 8}
        for p in range(q + 1, SUB):
            e = at(q, p)
            for i in col[p]:
                if i >= first + p // 8:
                    col[p][i] = col[p][i] - mult[i] * e
        here = first + q // 8
        for t in rows:
            e = spread(t[here], q % 8)
            for i in mult:
                if i > here:
                    t[i] = t[i] - mult[i] * e
                elif q % 8 < 7:
                    t[i] = t[i] - jnp.where(sub > q % 8, mult[i], 0.0) * e
    return [lax.rsqrt(v) for v in piv]


def factor_rows(rows, left):
    rows = [list(t) for t in rows]
    scales = []
    for first in range(0, len(rows[0]), 2):
        scales += eliminate(rows, left + first * 8, first)
    return [jnp.concatenate([v * s for v, s in zip(t, scales)], axis=0) for t in rows]


def block_at(a, b):
    return a * 4 - a * (a - 1) // 2 + b - a


def product(a, b):
    ah, am, al = split3(a)
    bh, bm, bl = split3(b)
    lhs = jnp.concatenate([ah, ah, am, ah, am, al], axis=1)
    rhs = jnp.concatenate([bh, bm, bh, bl, bm, bh], axis=0)
    return lax.dot_general(lhs, rhs, (((1,), (0,)), ((), ())), preferred_element_type=jnp.float32)


def cholesky_packed(g, inv, row, col):
    n = 4
    mine, own_strip = row // 8, row % 8 // (STRIP // 16)
    eye = (lax.broadcasted_iota(jnp.int32, (BLK, BLK), 0) == lax.broadcasted_iota(jnp.int32, (BLK, BLK), 1)).astype(jnp.float32)
    def panel(k, b):
        o = block_at(k, b) * BLK
        g[o:o + BLK, :] = product(inv[k % 2], g[o:o + BLK, :])

    def update(k, a, b):
        o, oa, ob = (block_at(*ab) * BLK for ab in ((a, b), (k, a), (k, b)))
        g[o:o + BLK, :] = g[o:o + BLK, :] - gram_like(g[oa:oa + BLK, :], g[ob:ob + BLK, :])

    def strip(k, refs, s, height=STRIP):
        at = s * STRIP
        tiles = [[r[o + at + i:o + at + i + 8, :] for i in range(0, height, 8)] for r, o in refs]
        done = factor_rows(tiles, at)
        for (r, o), v in zip(refs, done):
            r[o + at:o + at + height, :] = v
        if height < STRIP:
            return
        end = at + STRIP
        if end < BLK:
            both = jnp.concatenate(done, axis=1) if len(done) > 1 else done[0]
            upd = gram_like(done[0], both)
            for i, (r, o) in enumerate(refs):
                r[o + end:o + BLK, :] = r[o + end:o + BLK, :] - upd[end:, i * BLK:(i + 1) * BLK]

    def block_row(k):
        refs = [(g, block_at(k, k) * BLK)]
        if k < n - 1:
            inv[k % 2] = eye
            refs.append((inv.at[k % 2], 0))
        for s in range(BLK // STRIP):
            if k < n - 1:
                pl.when((mine - k) * (BLK // STRIP) + own_strip >= s)(functools.partial(strip, k, refs, s))
            else:
                pl.when(row % 8 > 2 * s)(functools.partial(strip, k, refs, s))
                pl.when(row % 8 == 2 * s)(functools.partial(strip, k, refs, s, STRIP // 2))
        for b in range(k + 1, n):
            panel(k, b)

        if k < n - 1:
            @pl.when(mine > k)
            def _():
                for a in range(k + 1, n):
                    for b in range(a, n):
                        update(k, a, b)

    @pl.when(col // 2 >= mine)
    def _():
        for k in range(n):
            pl.when(mine >= k)(functools.partial(block_row, k))


def own_part(g, row, col):
    a, b = row // 8, col // 2
    o = pl.multiple_of(block_at(a, b) * BLK + (row % 8) * 16, 16)
    v = g[pl.ds(o, 16), :]
    shifted = jnp.concatenate([v[:, 64:], v[:, :64]], axis=1)
    i = row * 16 + lax.broadcasted_iota(jnp.int32, (16, BLK), 0)
    j = col * 64 + lax.broadcasted_iota(jnp.int32, (16, BLK), 1)
    half = lax.broadcasted_iota(jnp.int32, (16, BLK), 1) * 0 + col % 2
    v = jnp.where(half == 1, shifted, v)
    return jnp.where(j >= i, v, 0.0)[:, :64]


def gram_body(cfg, tt_ref, ft_any, out_ref, ft_ref, tb, pf, sb, xb, gp, rc, hb, rx, zb, rz, gf, work, inv,
              ld_sem, sa_sem, ra_sem, sc_sem, rc_sem, sx_sem, rx_sem, sz_sem, rz_sem, sg_sem, rg_sem, ft_sem, col_sem):
    nx, ny, nz, jl, scale = cfg
    half = gp.shape[1]
    nq = nx * ny
    rows = half // nq
    g = lax.axis_index("grp")
    d = lax.axis_index("dev")
    x, c = g // 2, g % 2
    y, z = d // nz, d % nz
    q_own = x * ny + y

    def dev_id(gg, dd):
        return {"grp": gg, "dev": dd}

    ft_cp = pltpu.make_async_copy(ft_any, ft_ref, ft_sem)
    ft_cp.start()
    chunks = []
    for t in range(ny):
        cg = (y + t) % ny
        cp = pltpu.make_async_copy(tt_ref.at[:, pl.ds(pl.multiple_of(cg * BLK, BLK), BLK), :], tb.at[t], ld_sem.at[t])
        cp.start()
        chunks.append(cp)

    barrier = pltpu.get_barrier_semaphore()
    nbar = 0

    def sig(gg, dd):
        pl.semaphore_signal(barrier, inc=1, device_id=dev_id(gg, dd), device_id_type=MESH)

    for k in range(1, nz):
        sig(g, y * nz + (z + k) % nz)
        nbar += 1
    for kx in range(nx):
        for ky in range(ny):
            if (kx, ky) != (0, 0):
                sig(((x + kx) % nx) * 2 + c, ((y + ky) % ny) * nz + z)
                nbar += 1
    sig(x * 2 + 1 - c, d)
    nbar += 1

    zorder = sorted(range(nz), key=lambda k: (-min(k, nz - k), k))
    mine = pl.ds(pl.multiple_of(d * jl, jl), jl)
    jg = 256 // BLK
    sends = []
    ft_cp.wait()
    for t in range(ny):
        chunks[t].wait()

        def proj(i, carry):
            rhs = tb[t, pl.ds(i * jg, jg)].reshape(jg * BLK, tb.shape[-1])
            o = lax.dot_general(ft_ref[...], rhs, (((1,), (1,)), ((), ())), preferred_element_type=jnp.float32)
            for rg in range(nz):
                for jj in range(jg):
                    pf[pl.ds(pl.multiple_of(rg * jl * 8 + (i * jg + jj) * 8, 8), 8), :] = o[rg * 8:(rg + 1) * 8, jj * BLK:(jj + 1) * BLK]
            return carry

        lax.fori_loop(0, jl // jg, proj, 0)
        cg = (y + t) % ny
        for n, zo in enumerate(zorder):
            rg = (z + zo) % nz
            local = t == 0 and zo == 0
            for r in range(8):
                v = pf[pl.ds(pl.multiple_of(rg * jl * 8, 8) + r, jl, stride=8), :].astype(jnp.bfloat16)
                if local:
                    xb[mine, r * BLK:(r + 1) * BLK] = v
                else:
                    sb[t, n, :, r * BLK:(r + 1) * BLK] = v
            if t == 0 and n == 0:
                pl.semaphore_wait(barrier, nbar)
                for k in range(1, ny):
                    pl.semaphore_signal(col_sem.at[k], inc=1, device_id=dev_id(g, (y + k) % ny * nz + z), device_id_type=MESH)
            if t == 1 and n == 0:
                for k in range(1, ny):
                    pl.semaphore_wait(col_sem.at[k], 1)
            if not local:
                cp = pltpu.make_async_remote_copy(sb.at[t, n], xb.at[mine, :], sa_sem.at[t, n], ra_sem.at[d],
                                                  device_id=dev_id(g, cg * nz + rg), device_id_type=MESH)
                cp.start()
                sends.append(cp)

    partner = dev_id(x * 2 + 1 - c, d)

    def to_core(idx):
        at = pl.ds(pl.multiple_of(idx * (BLK // 2), BLK // 2), BLK // 2)
        return pltpu.make_async_remote_copy(gp.at[1 - c, at, :], rc.at[at, :], sc_sem.at[idx], rc_sem.at[idx],
                                            device_id=partner, device_id_type=MESH)

    for t in range(ny):
        ya = (y + ny - t) % ny
        for k in range(0 if t else 1, nz):
            src = ya * nz + (z + k) % nz
            landed = xb.at[pl.ds(pl.multiple_of(src * jl, jl), jl), :]
            pltpu.make_async_copy(landed, landed, ra_sem.at[src]).wait()

        def gram_block(u, carry, t=t):
            a = (y + ny - t) % ny
            b = (y + ny - u) % ny
            less = (b - a + ny - 1) // ny
            lo = b + (a - b) * less
            hi = a + b - lo
            idx = lo * 4 - lo * (lo - 1) // 2 + hi - lo
            xa = xb[pl.ds(pl.multiple_of(lo * BLK, BLK), BLK), :]
            xc = xb[pl.ds(pl.multiple_of(hi * BLK, BLK), BLK), :]
            o = lax.dot_general(xa, xc, (((1,), (1,)), ((), ())), preferred_element_type=jnp.float32) * scale
            at = pl.ds(pl.multiple_of(idx * (BLK // 2), BLK // 2), BLK // 2)
            gp[0, at, :] = o[:BLK // 2]
            gp[1, at, :] = o[BLK // 2:]
            to_core(idx).start()
            return carry

        lax.fori_loop(0, t + 1, gram_block, 0)
    own = pl.multiple_of(c * half, 8)
    other = pl.multiple_of((1 - c) * half, 8)
    for idx in range(10):
        to_core(idx).wait_recv()
    hb[...] = gp[c] + rc[...]

    plane = sorted(((kx, ky) for kx in range(nx) for ky in range(ny)), key=lambda k: min(k[0], nx - k[0]) + min(k[1], ny - k[1]))
    parts = []
    at_row = 0
    for n in PARTS:
        parts.append((at_row, n))
        at_row += n
    later = []

    def send(src, dst, s_sem, r_sem, to):
        cp = pltpu.make_async_remote_copy(src, dst, s_sem, r_sem, device_id=to, device_id_type=MESH)
        cp.start()
        later.append(cp)

    def at_peer(kx, ky):
        px, py = (x + kx) % nx, (y + ky) % ny
        return px * ny + py, dev_id(px * 2 + c, py * nz + z)

    def held(base, r0, n):
        return gf.at[pl.ds(pl.multiple_of(base + r0, 8), n), :]

    for p, (r0, n) in enumerate(parts):
        for kx, ky in plane[1:]:
            q, to = at_peer(kx, ky)
            send(hb.at[pl.ds(pl.multiple_of(q * rows + r0, 8), n), :], rx.at[q_own, pl.ds(r0, n)],
                 sx_sem.at[0, p, kx * ny + ky], rx_sem.at[0, p, q_own], to)
    rx[q_own] = hb[pl.ds(pl.multiple_of(q_own * rows, 8), rows), :]
    for p, (r0, n) in enumerate(parts):
        def wait_xy(k, carry, p=p, r0=r0, n=n):
            q = (q_own + k) % nq
            piece = rx.at[q, pl.ds(r0, n)]
            pltpu.make_async_copy(piece, piece, rx_sem.at[0, p, q]).wait()
            return carry

        lax.fori_loop(1, nq, wait_xy, 0)
        acc = rx[0, r0:r0 + n]
        for q in range(1, nq):
            acc += rx[q, r0:r0 + n]
        zb[r0:r0 + n] = acc
        for kz in range(1, nz):
            send(zb.at[pl.ds(r0, n)], rz.at[z, pl.ds(r0, n)], sz_sem.at[p, kz], rz_sem.at[p, z],
                 dev_id(g, y * nz + (z + kz) % nz))
        rz[z, r0:r0 + n] = acc
    for p, (r0, n) in enumerate(parts):
        for kz in range(1, nz):
            piece = rz.at[(z + kz) % nz, pl.ds(r0, n)]
            pltpu.make_async_copy(piece, piece, rz_sem.at[p, (z + kz) % nz]).wait()
        acc = rz[0, r0:r0 + n]
        for k in range(1, nz):
            acc += rz[k, r0:r0 + n]
        gf[pl.ds(pl.multiple_of(own + q_own * rows + r0, 8), n), :] = acc
        here = held(own + q_own * rows, r0, n)
        for kx, ky in plane[1:]:
            send(here, here, sx_sem.at[1, p, kx * ny + ky], rx_sem.at[1, p, q_own], at_peer(kx, ky)[1])
    for p, (r0, n) in enumerate(parts):
        for kx, ky in plane:
            q = at_peer(kx, ky)[0]
            piece = held(own + q * rows, r0, n)
            if (kx, ky) != (0, 0):
                pltpu.make_async_copy(piece, piece, rx_sem.at[1, p, q]).wait()
            send(piece, piece, sg_sem.at[p, q], rg_sem.at[p, q], partner)
    for p, (r0, n) in enumerate(parts):
        for q in range(nq):
            piece = held(other + q * rows, r0, n)
            pltpu.make_async_copy(piece, piece, rg_sem.at[p, q]).wait()
    hb_rows = BLK // 2
    for idx in range(10):
        for h in range(2):
            work[idx * BLK + h * hb_rows:idx * BLK + (h + 1) * hb_rows, :] = gf[h * half + idx * hb_rows:h * half + (idx + 1) * hb_rows, :]
    cholesky_packed(work, inv, d, g)
    out_ref[...] = own_part(work, d, g)
    for idx in range(10):
        to_core(idx).wait_send()
    for cp in sends + later:
        cp.wait_send()


def triangle(tt, ft, nx, ny, nz, scale):
    jl, ks, ni = tt.shape
    n2 = jl * ny * nz
    nq = nx * ny
    half = 5 * BLK
    rows = half // nq
    np_ = len(PARTS)
    cfg = (nx, ny, nz, jl, scale)
    f32, bf16 = jnp.float32, jnp.bfloat16
    dma = pltpu.SemaphoreType.DMA
    return pl.pallas_call(
        functools.partial(gram_body, cfg),
        out_shape=jax.ShapeDtypeStruct((n2 // (ny * nz), n2 // (2 * nx)), f32),
        in_specs=[pl.BlockSpec(memory_space=pltpu.MemorySpace.HBM)] * 2,
        out_specs=pl.BlockSpec(memory_space=pltpu.VMEM),
        scratch_shapes=[
            pltpu.VMEM(ft.shape, bf16),
            pltpu.VMEM((ny, jl, BLK, ni), bf16),
            pltpu.VMEM((nz * jl * 8, BLK), f32),
            pltpu.VMEM((ny, nz, jl, 8 * BLK), bf16),
            pltpu.VMEM((n2, 8 * BLK), bf16),
            pltpu.VMEM((2, half, BLK), f32),
            pltpu.VMEM((half, BLK), f32),
            pltpu.VMEM((half, BLK), f32),
            pltpu.VMEM((nq, rows, BLK), f32),
            pltpu.VMEM((rows, BLK), f32),
            pltpu.VMEM((nz, rows, BLK), f32),
            pltpu.VMEM((2 * half, BLK), f32),
            pltpu.VMEM((2 * half, BLK), f32),
            pltpu.VMEM((2, BLK, BLK), f32),
            dma((ny,)),
            dma((ny, nz)), dma((ny * nz,)),
            dma((10,)), dma((10,)),
            dma((2, np_, nq)), dma((2, np_, nq)),
            dma((np_, nz)), dma((np_, nz)),
            dma((np_, nq)), dma((np_, nq)),
            dma(()),
            pltpu.SemaphoreType.REGULAR((ny,)),
        ],
        compiler_params=pltpu.CompilerParams(collective_id=0, has_side_effects=True, vmem_limit_bytes=48 << 20),
    )(tt, ft)


def per_device(ny, tensor_slab, mode_factor):
    ni, jl, kl, s = tensor_slab.shape
    grp, dev = lax.axis_size("grp"), lax.axis_size("dev")
    tt = jnp.transpose(tensor_slab, (1, 2, 3, 0)).reshape(jl, kl * s, ni)
    row_total = mode_factor.shape[1] * kl * s * grp
    return triangle(tt, mode_factor.T, grp // 2, ny, dev // ny, 1.0 / row_total)


def solution(mesh, ny=NY):
    in_specs = (P(None, "dev", "grp", None), P())
    out_specs = P("dev", "grp")
    return jax.shard_map(
        functools.partial(per_device, ny), mesh=mesh, in_specs=in_specs, out_specs=out_specs, check_vma=False
    )
```
